128 devices in a mesh: rt: 32 (over x_lo, z, y), mob: 4 (over x_hi, core).
Axes of the slice: x: 4 (x_hi: 2, x_lo: 2; x = x_hi * 2 + x_lo), y: 4, z: 4, core: 2. Of those that a mesh axis runs over, the one named last changes fastest.
Arguments:
- observed: float32 [1024, 64, 1280], P('rt', 'mob'), as said below
- frame_kernel: float32 [31], replicated, may hold values from 0.05 to 1
- scan_kernel: float32 [15], replicated, may hold values from 0.05 to 1
- prec_window: int32 [256], P('rt'), may hold values from 0 to 15
- frag_window: int32 [1024], P('mob'), may hold values from 0 to 15
Outputs:
- estimate: float32 [1024, 64, 1280], P('rt', 'mob')
- correlation: float32 [256, 1024], P('rt', 'mob')
The draws below stay inside these ranges and needn't reach their ends.
Inputs may be any that keep to these rules, and one draw needn't show every extreme that they name: `observed`: positive intensities.
All inputs are finite; a program needn't handle non-finite values.
Results may differ from the reference program's by a relative error of at most 0.0003.
Values sent between devices are 32-bit elements; how exact they have to be, the bound alone decides.
No kernel may reach another device: no remote copies, remote signals or barrier semaphores. Data moves between devices by JAX's collectives and lax.ppermute only.
A program may use at most 64 MiB of HBM per device.

```python
import math
import jax
import jax.numpy as jnp
from jax import lax

PREC = 256
FRAG = 1024
KR = 31
KS = 15
ITERS = 2
WINDOWS = 16
F_DEV = 32
NF = 1024
NS = 64


def draw_observed(key, part):
    keys = jax.random.split(key, 3)
    channels = PREC + FRAG
    frames = jnp.arange(NF, dtype=jnp.float32)[:, None, None]
    center = jax.random.uniform(keys[0], (1, 1, channels), jnp.float32) * NF
    sigma = 2.0 * F_DEV
    peak = jnp.exp(-0.5 * ((frames - center) / sigma) ** 2)
    ramp = 1.0 + 2.0 * frames / NF
    noise = jnp.exp(jax.random.uniform(keys[1], (NF, NS, channels), jnp.float32, math.log(0.3), math.log(3.0)))
    scale = jnp.exp(jax.random.uniform(keys[2], (1, 1, channels), jnp.float32, math.log(0.5), math.log(4.0)))
    shape_part = 0.3 + 3.0 * peak
    return (scale * ramp * shape_part * noise).astype(jnp.float32)


def with_ends(entries, own_key, smallest, largest):
    index_at = [jax.random.randint(jax.random.fold_in(own_key, axis), (), 0, length) for axis, length in enumerate(entries.shape)]
    widest = entries.shape.index(max(entries.shape))
    next_to = index_at[:widest] + [(index_at[widest] + 1) % entries.shape[widest]] + index_at[widest + 1:]
    return entries.at[tuple(index_at)].set(smallest).at[tuple(next_to)].set(largest)


def setup_inputs(seed: int = 0) -> dict:
    streams_of = jax.random.split(jax.random.key(seed), 6)
    observed = draw_observed(jax.random.fold_in(streams_of[5], 71), 0)
    frame_kernel = jnp.clip(jnp.exp(jax.random.uniform(streams_of[1], (KR,), jnp.float32, math.log(0.05), math.log(1.0))), 0.05, 1.0)
    scan_kernel = jnp.clip(jnp.exp(jax.random.uniform(streams_of[2], (KS,), jnp.float32, math.log(0.05), math.log(1.0))), 0.05, 1.0)
    prec_window = with_ends(jax.random.randint(streams_of[3], (PREC,), 0, WINDOWS), jax.random.fold_in(streams_of[3], 1), 0, WINDOWS - 1).astype(jnp.int32)
    frag_window = with_ends(jax.random.randint(streams_of[4], (FRAG,), 0, WINDOWS), jax.random.fold_in(streams_of[4], 1), 0, WINDOWS - 1).astype(jnp.int32)
    return dict(observed=observed, frame_kernel=frame_kernel, scan_kernel=scan_kernel, prec_window=prec_window, frag_window=frag_window)


def blur_along(values, kernel, along):
    radius = (kernel.shape[0] - 1) // 2
    length = values.shape[along]
    widths = [(0, 0), (0, 0), (0, 0)]
    widths[along] = (radius, radius)
    padded = jnp.pad(values, widths)
    running = kernel[0] * lax.slice_in_dim(padded, 0, length, axis=along)
    for tap_index in range(1, kernel.shape[0]):
        running = running + kernel[tap_index] * lax.slice_in_dim(padded, tap_index, tap_index + length, axis=along)
    return running

def forward_blur(values, frame_kernel, scan_kernel):
    return blur_along(blur_along(values, scan_kernel, 1), frame_kernel, 0)

def adjoint_blur(values, frame_kernel, scan_kernel):
    return blur_along(blur_along(values, frame_kernel[::-1], 0), scan_kernel[::-1], 1)

def reference(observed, frame_kernel, scan_kernel, prec_window, frag_window):
    estimate = observed
    for iteration in range(ITERS):
        ratio_field = observed / forward_blur(estimate, frame_kernel, scan_kernel)
        estimate = estimate * adjoint_blur(ratio_field, frame_kernel, scan_kernel)
    profiles = estimate.reshape(NF * NS, PREC + FRAG)
    channel_mean = lax.optimization_barrier(jnp.sum(profiles, axis=0)) / (NF * NS)
    centered = (profiles - channel_mean).astype(jnp.bfloat16)
    as_float = centered.astype(jnp.float32)
    squares = lax.optimization_barrier(jnp.sum(as_float * as_float, axis=0))
    cross_sums = lax.dot_general(centered[:, :PREC], centered[:, PREC:], (((0,), (0,)), ((), ())), preferred_element_type=jnp.float32)
    inverse_norm = 1.0 / jnp.sqrt(squares + 1e-06)
    pair_mask = (prec_window[:, None] == frag_window[None, :]).astype(jnp.float32)
    correlation = pair_mask * cross_sums * inverse_norm[:PREC][:, None] * inverse_norm[PREC:][None, :]
    return (estimate, correlation)
```

```python
import functools

import jax
import jax.numpy as jnp
from jax import lax
from jax.experimental import pallas as pl
from jax.experimental.pallas import tpu as pltpu
from jax.sharding import PartitionSpec as P

PREC = 256
ITERS = 2
LANES = 128
AXES = ("rt", "mob")
BLOCK = 256
HALO = 128

F32 = jnp.float32
BF16 = jnp.bfloat16


def split(values):
    high = values.astype(BF16)
    return high, (values - high.astype(F32)).astype(BF16)


def taps_at(offset, taps_ref, count):
    out = jnp.zeros(offset.shape, F32)
    for tap in range(count):
        out = jnp.where(offset == tap, taps_ref[tap], out)
    return out


def frame_rows(scan, k, frames, scans, tiles):
    return pl.ds((scan // 8 * tiles + k) * 8 + scan % 8, frames, stride=scans * tiles)


def to_tiles(field):
    frames, scans, channels = field.shape
    field = field.reshape(frames, scans // 8, 8, channels // LANES, LANES).transpose(0, 1, 3, 2, 4)
    return field.reshape(frames * scans * channels // LANES, LANES)


def from_tiles(rows, frames, scans):
    tiles = rows.shape[0] // (frames * scans)
    field = rows.reshape(frames, scans // 8, tiles, 8, LANES).transpose(0, 1, 3, 2, 4)
    return field.reshape(frames, scans, tiles * LANES)


def pack_kernel(
    frame_ref, scan_ref, x_ref, p_ref, wf_ref, wa_ref, sf_ref, sa_ref, *, frames, scans, radii, group
):
    per_lane = LANES // frames
    quads = scans // per_lane
    owners = LANES
    rows = p_ref.shape[0] // owners
    tiles = x_ref.shape[0] // (frames * scans)

    def body(k, carry):
        for q in range(quads):
            block = jnp.concatenate(
                [x_ref[frame_rows(q * per_lane + j, k, frames, scans, tiles), :] for j in range(per_lane)], axis=0
            )
            p_ref[pl.ds(k * quads + q, owners, stride=rows), :] = block.T
        return carry

    lax.fori_loop(0, tiles, body, 0)

    frame_radius, scan_radius = radii
    source = lax.broadcasted_iota(jnp.int32, (BLOCK, BLOCK), 0)
    target = lax.broadcasted_iota(jnp.int32, (BLOCK, BLOCK), 1)
    edge = lax.broadcasted_iota(jnp.int32, (HALO, BLOCK), 0)
    edge = jnp.where(edge < HALO // 2, edge + BLOCK, edge - HALO)
    edge_target = lax.broadcasted_iota(jnp.int32, (HALO, BLOCK), 1)
    for ref, sign in ((wf_ref, 1), (wa_ref, -1)):
        high, low = split(taps_at(sign * (source - target) + frame_radius, frame_ref, 2 * frame_radius + 1))
        edge_high, edge_low = split(
            taps_at(sign * (edge - edge_target) + frame_radius, frame_ref, 2 * frame_radius + 1)
        )
        pieces = (high, high, low, edge_high, edge_high, edge_low)
        at = 0
        for piece in pieces:
            ref[at : at + piece.shape[0], :] = piece
            at += piece.shape[0]
    row = lax.broadcasted_iota(jnp.int32, (group, group), 0)
    col = lax.broadcasted_iota(jnp.int32, (group, group), 1)

    def place(index):
        tile, inner = index // 8, index % 8
        scan = (tile // per_lane) * scans + (inner % quads) * per_lane + tile % per_lane
        return scan, inner // quads

    row_scan, row_channel = place(row)
    col_scan, col_channel = place(col)
    for ref, sign in ((sf_ref, 1), (sa_ref, -1)):
        matrix = jnp.where(
            row_channel == col_channel,
            taps_at(sign * (col_scan - row_scan) + scan_radius, scan_ref, 2 * scan_radius + 1),
            0.0,
        )
        high, low = split(matrix)
        ref[:, 0:group] = high
        ref[:, group : 2 * group] = high
        ref[:, 2 * group : 3 * group] = low


def swap_blocks(tiles, lane, width):
    first, second, third, fourth = tiles
    wide = lane < 2 * width
    narrow = (lane % (2 * width)) < width
    pairs = []
    for a, b in ((first, third), (second, fourth)):
        pairs.append(
            (
                jnp.where(wide, a, pltpu.roll(b, 2 * width, 1)),
                jnp.where(wide, pltpu.roll(a, 2 * width, 1), b),
            )
        )
    out = []
    for a, b in zip(pairs[0], pairs[1]):
        out.append(jnp.where(narrow, a, pltpu.roll(b, width, 1)))
        out.append(jnp.where(narrow, pltpu.roll(a, LANES - width, 1), b))
    return out


def deblur_kernel(p_ref, wf_ref, wa_ref, sf_ref, sa_ref, out_ref, obs_ref, est_ref, mean_ref, *, frames, mobs, rows, cells):
    owners = LANES
    out_rows = out_ref.shape[0] // owners
    blocks, group, width = obs_ref.shape
    per_lane = LANES // frames
    lane = lax.broadcasted_iota(jnp.int32, (8, LANES), 1)
    row8 = lax.broadcasted_iota(jnp.int32, (8, 1), 0)
    halo_lane = lax.broadcasted_iota(jnp.int32, (group, HALO), 1)
    halves = width // LANES
    mean_ref[...] = jnp.zeros_like(mean_ref)

    def scan_blur(values, matrix):
        high, low = split(values)
        return jnp.dot(matrix, jnp.concatenate([high, low, high], axis=0), preferred_element_type=F32)

    def frame_blur(values, matrix):
        parts = [split(v) for v in values]
        lhs = []
        for n in range(blocks):
            center_high, center_low = parts[n]
            halo = []
            for which in (0, 1):
                after = parts[n + 1][which][:, :HALO] if n + 1 < blocks else None
                before = parts[n - 1][which][:, width - HALO :] if n else None
                zero = jnp.zeros((group, HALO), BF16)
                halo.append(
                    jnp.where(
                        halo_lane < HALO // 2,
                        zero if after is None else after,
                        zero if before is None else before,
                    )
                )
            lhs.append(
                jnp.concatenate([center_high, center_low, center_high, halo[0], halo[1], halo[0]], axis=1)
            )
        out = jnp.dot(jnp.concatenate(lhs, axis=0), matrix, preferred_element_type=F32)
        return [out[n * group : (n + 1) * group] for n in range(blocks)]

    def total8(parts):
        acc = None
        for part in parts:
            for half in range(halves):
                piece = part[:, half * LANES : (half + 1) * LANES].reshape(group // 8, 8, LANES).sum(axis=0)
                acc = piece if acc is None else acc + piece
        rows_sum = jnp.sum(acc, axis=1, keepdims=True)
        zero = jnp.zeros_like(rows_sum)
        upper = jnp.sum(jnp.where(row8 < 4, rows_sum, zero), axis=0, keepdims=True)
        lower = jnp.sum(jnp.where(row8 < 4, zero, rows_sum), axis=0, keepdims=True)
        return upper, lower

    def body(pair, carry):
        def at(run, y, mob, stride):
            start = ((run * per_lane + y) * mobs + mob) * stride + pair * 8
            return pl.ds(pl.multiple_of(start, 8), 8)

        for run in range(blocks * halves):
            n, half = run // halves, run % halves
            for mob in range(mobs):
                tiles = [p_ref[at(run, y, mob, rows), :] for y in range(per_lane)]
                for j, tile in enumerate(swap_blocks(tiles, lane, frames)):
                    b = mob * per_lane + j
                    obs_ref[n, b * 8 : b * 8 + 8, half * LANES : (half + 1) * LANES] = tile
                    est_ref[n, b * 8 : b * 8 + 8, half * LANES : (half + 1) * LANES] = tile

        for _ in range(ITERS):
            blurred = frame_blur([scan_blur(est_ref[n], sf_ref[...]) for n in range(blocks)], wf_ref[...])
            ratio = [obs_ref[n] / blurred[n] for n in range(blocks)]
            back = frame_blur(ratio, wa_ref[...])
            for n in range(blocks):
                est_ref[n] = est_ref[n] * scan_blur(back[n], sa_ref[...])

        upper, lower = total8([est_ref[n] for n in range(blocks)])
        upper_mean, lower_mean = upper / cells, lower / cells
        mean8 = jnp.where(row8 < 4, upper_mean, lower_mean)
        squares = []
        for n in range(blocks):
            centered = est_ref[n].reshape(group // 8, 8, width) - mean8[None]
            centered = centered.astype(BF16).astype(F32).reshape(group, width)
            squares.append(centered * centered)
        upper_sq, lower_sq = total8(squares)
        upper_inv = 1.0 / jnp.sqrt(upper_sq + 1e-06)
        lower_inv = 1.0 / jnp.sqrt(lower_sq + 1e-06)
        held = mean_ref[...]
        held = jnp.where(lane == 2 * pair, upper_mean, held)
        held = jnp.where(lane == 2 * pair + 1, lower_mean, held)
        held = jnp.where(lane == LANES // 2 + 2 * pair, upper_inv, held)
        held = jnp.where(lane == LANES // 2 + 2 * pair + 1, lower_inv, held)
        mean_ref[...] = held

        for run in range(blocks * halves):
            n, half = run // halves, run % halves
            for mob in range(mobs):
                tiles = []
                for j in range(per_lane):
                    b = mob * per_lane + j
                    tiles.append(est_ref[n, b * 8 : b * 8 + 8, half * LANES : (half + 1) * LANES])
                for y, tile in enumerate(swap_blocks(tiles, lane, frames)):
                    out_ref[at(run, y, mob, out_rows), :] = tile
        return carry

    lax.fori_loop(0, rows // 8, body, 0)
    for owner in range(owners):
        out_ref[owner * out_rows + rows : owner * out_rows + rows + 8, :] = mean_ref[...]


def unpack_kernel(q_ref, est_ref, cross_ref, centered_ref, *, frames, scans, rows, shards):
    owners = LANES
    stride = q_ref.shape[0] // owners
    per_lane = LANES // frames
    quads = scans // per_lane
    channels = centered_ref.shape[1]
    tiles = channels // LANES
    stats = q_ref[pl.ds(rows, owners, stride=stride), :]
    stats_t = stats.T
    for k in range(channels // LANES):
        lanes = slice(k * LANES, (k + 1) * LANES)
        for q in range(quads):
            block = q_ref[pl.ds(k * quads + q, owners, stride=stride), :].T
            for j in range(per_lane):
                est_ref[frame_rows(q * per_lane + j, k, frames, scans, tiles), :] = block[j * frames : (j + 1) * frames]
            centered_ref[q * LANES : (q + 1) * LANES, lanes] = (block - stats_t[k : k + 1]).astype(BF16)
    row_shards, column_shards = shards
    wide = (channels - PREC) // column_shards
    for m in range(column_shards):
        cross = lax.dot_general(
            centered_ref[:, :PREC],
            centered_ref[:, PREC + m * wide : PREC + (m + 1) * wide],
            (((0,), (0,)), ((), ())),
            preferred_element_type=F32,
        )
        first = (PREC + m * wide) // LANES
        column = jnp.concatenate(
            [stats_t[LANES // 2 + first + i : LANES // 2 + first + i + 1] for i in range(wide // LANES)], axis=1
        )
        row = jnp.concatenate(
            [stats[:, LANES // 2 + k : LANES // 2 + k + 1] for k in range(PREC // LANES)], axis=0
        )
        cross = cross * row * column
        cross_ref[:, m] = cross.reshape(row_shards, PREC // row_shards, wide)


def local(observed, frame_kernel, scan_kernel, prec_window, frag_window):
    frames, scans, channels = observed.shape
    row_shards, mobs = lax.axis_size("rt"), lax.axis_size("mob")
    owners = row_shards * mobs
    per_lane = LANES // frames
    quads = scans // per_lane
    rows = channels // owners * quads
    group = 8 * per_lane * mobs
    blocks = row_shards * frames // BLOCK
    out_rows = rows + 8
    width = (channels - PREC) // mobs
    vmem = pl.BlockSpec(memory_space=pltpu.VMEM)
    smem = pl.BlockSpec(memory_space=pltpu.SMEM)
    depth = 3 * BLOCK + 3 * HALO
    radii = ((frame_kernel.shape[0] - 1) // 2, (scan_kernel.shape[0] - 1) // 2)
    packed, wf, wa, sf, sa = pl.pallas_call(
        functools.partial(pack_kernel, frames=frames, scans=scans, radii=radii, group=group),
        out_shape=(
            jax.ShapeDtypeStruct((owners * rows, LANES), F32),
            jax.ShapeDtypeStruct((depth, BLOCK), BF16),
            jax.ShapeDtypeStruct((depth, BLOCK), BF16),
            jax.ShapeDtypeStruct((group, 3 * group), BF16),
            jax.ShapeDtypeStruct((group, 3 * group), BF16),
        ),
        in_specs=[smem, smem, vmem],
        out_specs=[vmem] * 5,
        name="pack",
    )(frame_kernel, scan_kernel, to_tiles(observed))
    arrived = lax.all_to_all(packed.reshape(owners, rows, LANES), AXES, 0, 0, tiled=True)
    deblurred = pl.pallas_call(
        functools.partial(
            deblur_kernel, frames=frames, mobs=mobs, rows=rows, cells=frames * scans * owners
        ),
        out_shape=jax.ShapeDtypeStruct((owners * out_rows, LANES), F32),
        in_specs=[vmem] * 5,
        out_specs=vmem,
        scratch_shapes=[
            pltpu.VMEM((blocks, group, BLOCK), F32),
            pltpu.VMEM((blocks, group, BLOCK), F32),
            pltpu.VMEM((8, LANES), F32),
        ],
        name="deblur",
    )(arrived.reshape(owners * rows, LANES), wf, wa, sf, sa)
    returned = lax.all_to_all(deblurred.reshape(owners, out_rows, LANES), AXES, 0, 0, tiled=True)
    estimate, cross = pl.pallas_call(
        functools.partial(
            unpack_kernel, frames=frames, scans=scans, rows=rows, shards=(row_shards, mobs)
        ),
        out_shape=(
            jax.ShapeDtypeStruct((frames * scans * channels // LANES, LANES), F32),
            jax.ShapeDtypeStruct((row_shards, mobs, PREC // row_shards, width), F32),
        ),
        in_specs=[vmem],
        out_specs=[vmem] * 2,
        scratch_shapes=[pltpu.VMEM((frames * scans, channels), BF16)],
        name="unpack",
    )(returned.reshape(owners * out_rows, LANES))
    sums = lax.all_to_all(cross.reshape(owners, PREC // row_shards, width), AXES, 0, 0, tiled=True)
    pair_mask = (prec_window[:, None] == frag_window[None, :]).astype(F32)
    correlation = pair_mask * jnp.sum(sums, axis=0)
    return from_tiles(estimate, frames, scans), correlation


def solution(mesh):
    placed = (P("rt", "mob", None), P(), P(), P("rt"), P("mob"))
    return jax.shard_map(
        local,
        mesh=mesh,
        in_specs=placed,
        out_specs=(P("rt", "mob", None), P("rt", "mob")),
        check_vma=False,
    )
```

```python
import functools

import jax
import jax.numpy as jnp
from jax import lax
from jax.experimental import pallas as pl
from jax.experimental.pallas import tpu as pltpu
from jax.sharding import PartitionSpec as P

PREC = 256
ITERS = 2
LANES = 128
AXES = ("rt", "mob")
BLOCK = 256
STATS = 2
HALO = 128

F32 = jnp.float32
BF16 = jnp.bfloat16


def split(values):
    high = values.astype(BF16)
    return high, (values - high.astype(F32)).astype(BF16)


def taps_at(offset, taps_ref, count):
    out = jnp.zeros(offset.shape, F32)
    for tap in range(count):
        out = jnp.where(offset == tap, taps_ref[tap], out)
    return out


def frame_rows(scan, k, frames, scans, tiles):
    return pl.ds((scan // 8 * tiles + k) * 8 + scan % 8, frames, stride=scans * tiles)


def to_tiles(field):
    frames, scans, channels = field.shape
    field = field.reshape(frames, scans // 8, 8, channels // LANES, LANES).transpose(0, 1, 3, 2, 4)
    return field.reshape(frames * scans * channels // LANES, LANES)


def from_tiles(rows, frames, scans):
    tiles = rows.shape[0] // (frames * scans)
    field = rows.reshape(frames, scans // 8, tiles, 8, LANES).transpose(0, 1, 3, 2, 4)
    return field.reshape(frames, scans, tiles * LANES)


def pack_kernel(x_ref, p_ref, *, frames, scans):
    per_lane = LANES // frames
    quads = scans // per_lane
    owners = LANES
    rows = p_ref.shape[0] // owners
    tiles = x_ref.shape[0] // (frames * scans)

    def body(k, carry):
        for q in range(quads):
            block = jnp.concatenate(
                [x_ref[frame_rows(q * per_lane + j, k, frames, scans, tiles), :] for j in range(per_lane)], axis=0
            )
            p_ref[pl.ds(k * quads + q, owners, stride=rows), :] = block.T
        return carry

    lax.fori_loop(0, tiles, body, 0)


def bands_kernel(frame_ref, scan_ref, wf_ref, wa_ref, sf_ref, sa_ref, *, scans, per_lane):
    frame_radius, scan_radius = (frame_ref.shape[0] - 1) // 2, (scan_ref.shape[0] - 1) // 2
    quads = scans // per_lane
    group = sf_ref.shape[0]
    source = lax.broadcasted_iota(jnp.int32, (BLOCK, BLOCK), 0)
    target = lax.broadcasted_iota(jnp.int32, (BLOCK, BLOCK), 1)
    edge = lax.broadcasted_iota(jnp.int32, (HALO, BLOCK), 0)
    edge = jnp.where(edge < HALO // 2, edge + BLOCK, edge - HALO)
    edge_target = lax.broadcasted_iota(jnp.int32, (HALO, BLOCK), 1)
    for ref, sign in ((wf_ref, 1), (wa_ref, -1)):
        high, low = split(taps_at(sign * (source - target) + frame_radius, frame_ref, 2 * frame_radius + 1))
        edge_high, edge_low = split(
            taps_at(sign * (edge - edge_target) + frame_radius, frame_ref, 2 * frame_radius + 1)
        )
        pieces = (high, high, low, edge_high, edge_high, edge_low)
        at = 0
        for piece in pieces:
            ref[at : at + piece.shape[0], :] = piece
            at += piece.shape[0]
    row = lax.broadcasted_iota(jnp.int32, (group, group), 0)
    col = lax.broadcasted_iota(jnp.int32, (group, group), 1)

    def place(index):
        tile, inner = index // 8, index % 8
        scan = (tile // per_lane) * scans + (inner % quads) * per_lane + tile % per_lane
        return scan, inner // quads

    row_scan, row_channel = place(row)
    col_scan, col_channel = place(col)
    for ref, sign in ((sf_ref, 1), (sa_ref, -1)):
        matrix = jnp.where(
            row_channel == col_channel,
            taps_at(sign * (col_scan - row_scan) + scan_radius, scan_ref, 2 * scan_radius + 1),
            0.0,
        )
        high, low = split(matrix)
        ref[:, 0:group] = high
        ref[:, group : 2 * group] = high
        ref[:, 2 * group : 3 * group] = low


def swap_blocks(tiles, lane, width):
    first, second, third, fourth = tiles
    wide = lane < 2 * width
    narrow = (lane % (2 * width)) < width
    pairs = []
    for a, b in ((first, third), (second, fourth)):
        pairs.append(
            (
                jnp.where(wide, a, pltpu.roll(b, 2 * width, 1)),
                jnp.where(wide, pltpu.roll(a, 2 * width, 1), b),
            )
        )
    out = []
    for a, b in zip(pairs[0], pairs[1]):
        out.append(jnp.where(narrow, a, pltpu.roll(b, width, 1)))
        out.append(jnp.where(narrow, pltpu.roll(a, LANES - width, 1), b))
    return out


def deblur_kernel(p_ref, wf_ref, wa_ref, sf_ref, sa_ref, out_ref, obs_ref, est_ref, mean_ref, *, frames, mobs, rows, cells):
    owners = LANES
    out_rows = out_ref.shape[0] // owners
    blocks, group, width = obs_ref.shape
    per_lane = LANES // frames
    lane = lax.broadcasted_iota(jnp.int32, (8, LANES), 1)
    row8 = lax.broadcasted_iota(jnp.int32, (8, 1), 0)
    halo_lane = lax.broadcasted_iota(jnp.int32, (group, HALO), 1)
    halves = width // LANES
    mean_ref[...] = jnp.zeros_like(mean_ref)

    def scan_blur(values, matrix):
        high, low = split(values)
        return jnp.dot(matrix, jnp.concatenate([high, low, high], axis=0), preferred_element_type=F32)

    def frame_blur(values, matrix):
        parts = [split(v) for v in values]
        lhs = []
        for n in range(blocks):
            center_high, center_low = parts[n]
            halo = []
            for which in (0, 1):
                after = parts[n + 1][which][:, :HALO] if n + 1 < blocks else None
                before = parts[n - 1][which][:, width - HALO :] if n else None
                zero = jnp.zeros((group, HALO), BF16)
                halo.append(
                    jnp.where(
                        halo_lane < HALO // 2,
                        zero if after is None else after,
                        zero if before is None else before,
                    )
                )
            lhs.append(
                jnp.concatenate([center_high, center_low, center_high, halo[0], halo[1], halo[0]], axis=1)
            )
        out = jnp.dot(jnp.concatenate(lhs, axis=0), matrix, preferred_element_type=F32)
        return [out[n * group : (n + 1) * group] for n in range(blocks)]

    def total8(parts):
        acc = None
        for part in parts:
            for half in range(halves):
                piece = part[:, half * LANES : (half + 1) * LANES].reshape(group // 8, 8, LANES).sum(axis=0)
                acc = piece if acc is None else acc + piece
        rows_sum = jnp.sum(acc, axis=1, keepdims=True)
        zero = jnp.zeros_like(rows_sum)
        upper = jnp.sum(jnp.where(row8 < 4, rows_sum, zero), axis=0, keepdims=True)
        lower = jnp.sum(jnp.where(row8 < 4, zero, rows_sum), axis=0, keepdims=True)
        return upper, lower

    def body(pair, carry):
        def at(run, y, mob, stride):
            start = ((run * per_lane + y) * mobs + mob) * stride + pair * 8
            return pl.ds(pl.multiple_of(start, 8) if stride % 8 == 0 else start, 8)

        for run in range(blocks * halves):
            n, half = run // halves, run % halves
            for mob in range(mobs):
                tiles = [p_ref[at(run, y, mob, rows), :] for y in range(per_lane)]
                for j, tile in enumerate(swap_blocks(tiles, lane, frames)):
                    b = mob * per_lane + j
                    obs_ref[n, b * 8 : b * 8 + 8, half * LANES : (half + 1) * LANES] = tile
                    est_ref[n, b * 8 : b * 8 + 8, half * LANES : (half + 1) * LANES] = tile

        for _ in range(ITERS):
            blurred = frame_blur([scan_blur(est_ref[n], sf_ref[...]) for n in range(blocks)], wf_ref[...])
            ratio = [obs_ref[n] / blurred[n] for n in range(blocks)]
            back = frame_blur(ratio, wa_ref[...])
            for n in range(blocks):
                est_ref[n] = est_ref[n] * scan_blur(back[n], sa_ref[...])

        upper, lower = total8([est_ref[n] for n in range(blocks)])
        upper_mean, lower_mean = upper / cells, lower / cells
        mean8 = jnp.where(row8 < 4, upper_mean, lower_mean)
        squares = []
        for n in range(blocks):
            centered = est_ref[n].reshape(group // 8, 8, width) - mean8[None]
            centered = centered.astype(BF16).astype(F32).reshape(group, width)
            squares.append(centered * centered)
        upper_sq, lower_sq = total8(squares)
        upper_inv = 1.0 / jnp.sqrt(upper_sq + 1e-06)
        lower_inv = 1.0 / jnp.sqrt(lower_sq + 1e-06)
        held = mean_ref[...]
        held = jnp.where(lane == 2 * pair, upper_mean, held)
        held = jnp.where(lane == 2 * pair + 1, lower_mean, held)
        held = jnp.where(lane == LANES // 2 + 2 * pair, upper_inv, held)
        held = jnp.where(lane == LANES // 2 + 2 * pair + 1, lower_inv, held)
        mean_ref[...] = held

        for run in range(blocks * halves):
            n, half = run // halves, run % halves
            for mob in range(mobs):
                tiles = []
                for j in range(per_lane):
                    b = mob * per_lane + j
                    tiles.append(est_ref[n, b * 8 : b * 8 + 8, half * LANES : (half + 1) * LANES])
                for y, tile in enumerate(swap_blocks(tiles, lane, frames)):
                    out_ref[at(run, y, mob, out_rows), :] = tile
        return carry

    lax.fori_loop(0, rows // 8, body, 0)
    for owner in range(owners):
        out_ref[owner * out_rows + rows : (owner + 1) * out_rows, :] = mean_ref[0:STATS, :]


def cross_kernel(q_ref, cross_ref, centered_ref, *, quads):
    owners = LANES
    stride = q_ref.shape[0] // owners
    channels = centered_ref.shape[0]
    tiles = channels // LANES
    row_shards, column_shards, shard_rows, wide = cross_ref.shape
    stats = q_ref[pl.ds(tiles * quads, owners, stride=stride), :]
    stats_t = stats.T
    for k in range(tiles):
        mean = jnp.broadcast_to(stats[:, k : k + 1], (owners, LANES))
        for q in range(quads):
            block = q_ref[pl.ds(k * quads + q, owners, stride=stride), :]
            centered_ref[k * LANES : (k + 1) * LANES, q * LANES : (q + 1) * LANES] = (block - mean).astype(BF16)
    row = jnp.concatenate([stats[:, LANES // 2 + k : LANES // 2 + k + 1] for k in range(PREC // LANES)], axis=0)
    for m in range(column_shards):
        cross = lax.dot_general(
            centered_ref[:PREC, :],
            centered_ref[PREC + m * wide : PREC + (m + 1) * wide, :],
            (((1,), (1,)), ((), ())),
            preferred_element_type=F32,
        )
        first = LANES // 2 + (PREC + m * wide) // LANES
        column = jnp.concatenate([stats_t[first + i : first + i + 1] for i in range(wide // LANES)], axis=1)
        cross_ref[:, m] = (cross * row * column).reshape(row_shards, shard_rows, wide)


def unpack_kernel(q_ref, est_ref, *, frames, scans):
    owners = LANES
    stride = q_ref.shape[0] // owners
    per_lane = LANES // frames
    quads = scans // per_lane
    tiles = est_ref.shape[0] // (frames * scans)

    def body(k, carry):
        for q in range(quads):
            block = q_ref[pl.ds(k * quads + q, owners, stride=stride), :].T
            for j in range(per_lane):
                est_ref[frame_rows(q * per_lane + j, k, frames, scans, tiles), :] = block[j * frames : (j + 1) * frames]
        return carry

    lax.fori_loop(0, tiles, body, 0)


def local(observed, frame_kernel, scan_kernel, prec_window, frag_window):
    frames, scans, channels = observed.shape
    row_shards, mobs = lax.axis_size("rt"), lax.axis_size("mob")
    owners = row_shards * mobs
    per_lane = LANES // frames
    quads = scans // per_lane
    rows = channels // owners * quads
    group = 8 * per_lane * mobs
    blocks = row_shards * frames // BLOCK
    out_rows = rows + STATS
    width = (channels - PREC) // mobs
    vmem = pl.BlockSpec(memory_space=pltpu.VMEM)
    smem = pl.BlockSpec(memory_space=pltpu.SMEM)
    depth = 3 * BLOCK + 3 * HALO

    def call(kernel, name, out_shape, specs, scratch=(), mib=16, micros=5, **statics):
        return pl.pallas_call(
            functools.partial(kernel, **statics),
            out_shape=out_shape,
            in_specs=specs,
            out_specs=jax.tree.map(lambda _: vmem, out_shape),
            scratch_shapes=scratch,
            compiler_params=pltpu.CompilerParams(vmem_limit_bytes=mib << 20),
            cost_estimate=pl.CostEstimate(
                flops=micros * 10**9, bytes_accessed=micros * 3 * 10**6, transcendentals=0
            ),
            name=name,
        )

    shape = jax.ShapeDtypeStruct
    cells = frames * scans
    packed = call(
        pack_kernel, "pack", shape((owners * rows, LANES), F32), [vmem], frames=frames, scans=scans
    )(to_tiles(observed))
    bands = call(
        bands_kernel,
        "bands",
        (shape((depth, BLOCK), BF16),) * 2 + (shape((group, 3 * group), BF16),) * 2,
        [smem, smem],
        scans=scans,
        per_lane=per_lane,
    )(frame_kernel, scan_kernel)
    arrived = lax.all_to_all(packed.reshape(owners, rows, LANES), AXES, 0, 0, tiled=True)
    deblurred = call(
        deblur_kernel,
        "deblur",
        shape((owners * out_rows, LANES), F32),
        [vmem] * 5,
        [
            pltpu.VMEM((blocks, group, BLOCK), F32),
            pltpu.VMEM((blocks, group, BLOCK), F32),
            pltpu.VMEM((8, LANES), F32),
        ],
        mib=24,
        frames=frames,
        mobs=mobs,
        rows=rows,
        cells=cells * owners,
    )(arrived.reshape(owners * rows, LANES), *bands)
    returned = lax.all_to_all(
        deblurred.reshape(owners, out_rows // STATS, STATS, LANES), AXES, 0, 0, tiled=True
    ).reshape(owners * out_rows, LANES)
    cross = call(
        cross_kernel,
        "cross",
        shape((row_shards, mobs, PREC // row_shards, width), F32),
        [vmem],
        [pltpu.VMEM((channels, cells), BF16)],
        quads=quads,
    )(returned)
    sums = lax.all_to_all(cross.reshape(owners, PREC // row_shards, width), AXES, 0, 0, tiled=True)
    estimate = call(
        unpack_kernel, "unpack", shape((cells * channels // LANES, LANES), F32), [vmem], frames=frames, scans=scans
    )(returned)
    pair_mask = (prec_window[:, None] == frag_window[None, :]).astype(F32)
    correlation = pair_mask * jnp.sum(sums, axis=0)
    return from_tiles(estimate, frames, scans), correlation


def solution(mesh):
    placed = (P("rt", "mob", None), P(), P(), P("rt"), P("mob"))
    return jax.shard_map(
        local,
        mesh=mesh,
        in_specs=placed,
        out_specs=(P("rt", "mob", None), P("rt", "mob")),
        check_vma=False,
    )
```

```python
import functools

import jax
import jax.numpy as jnp
from jax import lax
from jax.experimental import pallas as pl
from jax.experimental.pallas import tpu as pltpu
from jax.sharding import PartitionSpec as P

PREC = 256
ITERS = 2
LANES = 128
AXES = ("rt", "mob")
BLOCK = 256
EDGE = 16
TOGETHER = 2
STATS = 2
HALO = 128

F32 = jnp.float32
BF16 = jnp.bfloat16


def split(values):
    high = values.astype(BF16)
    return high, (values - high.astype(F32)).astype(BF16)


def taps_at(offset, taps_ref, count):
    out = jnp.zeros(offset.shape, F32)
    for tap in range(count):
        out = jnp.where(offset == tap, taps_ref[tap], out)
    return out


def frame_rows(scan, k, frames, scans, tiles):
    return pl.ds((scan // 8 * tiles + k) * 8 + scan % 8, frames, stride=scans * tiles)


def to_tiles(field):
    frames, scans, channels = field.shape
    field = field.reshape(frames, scans // 8, 8, channels // LANES, LANES).transpose(0, 1, 3, 2, 4)
    return field.reshape(frames * scans // 8, channels // LANES, 8, LANES)


def from_tiles(rows, frames, scans):
    tiles = rows.shape[0] // (frames * scans)
    field = rows.reshape(frames, scans // 8, tiles, 8, LANES).transpose(0, 1, 3, 2, 4)
    return field.reshape(frames, scans, tiles * LANES)


def pack_kernel(x_hbm, p_hbm, x_ref, p_ref, in_sem, out_sem, *, frames, scans):
    per_lane = LANES // frames
    quads = scans // per_lane
    owners, rows = LANES, p_ref.shape[0] // LANES
    tiles = x_ref.shape[0]
    steps = rows // 8
    each = tiles // steps

    def arrive(k):
        return pltpu.make_async_copy(x_hbm.at[:, k], x_ref.at[k], in_sem.at[k])

    def leave(step):
        here = pl.ds(pl.multiple_of(step * 8, 8), 8)
        return pltpu.make_async_copy(
            p_ref.reshape(owners, rows, LANES).at[:, here], p_hbm.at[:, here], out_sem.at[step]
        )

    for k in range(tiles):
        arrive(k).start()

    def body(step, carry):
        for sub in range(each):
            k = step * each + sub
            arrive(k).wait()
            view = x_ref.at[k].reshape(frames * scans, LANES)
            for q in range(quads):
                block = jnp.concatenate(
                    [view[pl.ds(q * per_lane + j, frames, stride=scans), :] for j in range(per_lane)], axis=0
                )
                p_ref[pl.ds(k * quads + q, owners, stride=rows), :] = block.T
        leave(step).start()
        return carry

    lax.fori_loop(0, steps, body, 0)
    for step in range(steps):
        leave(step).wait()


def bands_kernel(frame_ref, scan_ref, wf_ref, wa_ref, sf_ref, sa_ref, *, scans, per_lane):
    frame_radius, scan_radius = (frame_ref.shape[0] - 1) // 2, (scan_ref.shape[0] - 1) // 2
    quads = scans // per_lane
    group = sf_ref.shape[0] // 2
    source = lax.broadcasted_iota(jnp.int32, (BLOCK, BLOCK), 0)
    target = lax.broadcasted_iota(jnp.int32, (BLOCK, BLOCK), 1)
    edge_row = lax.broadcasted_iota(jnp.int32, (HALO, BLOCK), 0)
    edge = jnp.where(edge_row < HALO // 2, edge_row + BLOCK, edge_row - HALO)
    again = (edge_row >= EDGE) & (edge_row < 3 * EDGE)
    edge_again = jnp.where(edge_row < 2 * EDGE, edge_row - 2 * EDGE, edge_row - 2 * EDGE + BLOCK)
    edge_target = lax.broadcasted_iota(jnp.int32, (HALO, BLOCK), 1)
    for ref, sign in ((wf_ref, 1), (wa_ref, -1)):
        high, low = split(taps_at(sign * (source - target) + frame_radius, frame_ref, 2 * frame_radius + 1))
        edge_high, _ = split(
            taps_at(sign * (edge - edge_target) + frame_radius, frame_ref, 2 * frame_radius + 1)
        )
        _, edge_low = split(
            taps_at(sign * (edge_again - edge_target) + frame_radius, frame_ref, 2 * frame_radius + 1)
        )
        pieces = (high, high, low, jnp.where(again, edge_low, edge_high), edge_high)
        at = 0
        for piece in pieces:
            ref[at : at + piece.shape[0], :] = piece
            at += piece.shape[0]
    row = lax.broadcasted_iota(jnp.int32, (group, group), 0)
    col = lax.broadcasted_iota(jnp.int32, (group, group), 1)

    def place(index):
        tile, inner = index // 8, index % 8
        scan = (tile // per_lane) * scans + (inner % quads) * per_lane + tile % per_lane
        return scan, inner // quads

    row_scan, row_channel = place(row)
    col_scan, col_channel = place(col)
    for ref, sign in ((sf_ref, 1), (sa_ref, -1)):
        matrix = jnp.where(
            row_channel == col_channel,
            taps_at(sign * (col_scan - row_scan) + scan_radius, scan_ref, 2 * scan_radius + 1),
            0.0,
        )
        high, low = split(matrix)
        ref[0:group, 0:group] = high
        ref[0:group, group : 2 * group] = high
        ref[group : 2 * group, 0:group] = low
        ref[group : 2 * group, group : 2 * group] = jnp.zeros_like(low)


def swap_blocks(tiles, lane, width):
    first, second, third, fourth = tiles
    wide = lane < 2 * width
    narrow = (lane % (2 * width)) < width
    pairs = []
    for a, b in ((first, third), (second, fourth)):
        pairs.append(
            (
                jnp.where(wide, a, pltpu.roll(b, 2 * width, 1)),
                jnp.where(wide, pltpu.roll(a, 2 * width, 1), b),
            )
        )
    out = []
    for a, b in zip(pairs[0], pairs[1]):
        out.append(jnp.where(narrow, a, pltpu.roll(b, width, 1)))
        out.append(jnp.where(narrow, pltpu.roll(a, LANES - width, 1), b))
    return out


def deblur_kernel(
    p_ref, wf_hbm, wa_hbm, sf_hbm, sa_hbm, out_ref,
    wf_ref, wa_ref, sf_ref, sa_ref, obs_ref, est_ref, left_ref, back_ref, mean_ref, band_sem,
    *, frames, mobs, rows, cells,
):
    copies = [
        pltpu.make_async_copy(source, target, band_sem.at[i])
        for i, (source, target) in enumerate(
            ((sf_hbm, sf_ref), (wf_hbm, wf_ref), (wa_hbm, wa_ref), (sa_hbm, sa_ref))
        )
    ]
    for copy in copies:
        copy.start()
    owners = LANES
    out_rows = out_ref.shape[0] // owners
    units, blocks, group, width = obs_ref.shape
    per_lane = LANES // frames
    lane = lax.broadcasted_iota(jnp.int32, (8, LANES), 1)
    row8 = lax.broadcasted_iota(jnp.int32, (8, 1), 0)
    halo_lane = lax.broadcasted_iota(jnp.int32, (group, HALO), 1)
    halves = width // LANES

    def at(pair, run, y, mob, stride):
        start = ((run * per_lane + y) * mobs + mob) * stride + pair * 8
        return pl.ds(start, 8)

    def scan_blur(values, matrix):
        high, low = split(values)
        both = jnp.dot(matrix, jnp.concatenate([high, low], axis=0), preferred_element_type=F32)
        return both[0:group] + both[group : 2 * group]

    def put(ref, u, n, values):
        high, low = split(values)
        ref[u, n * group : (n + 1) * group, 0:width] = high
        ref[u, n * group : (n + 1) * group, width : 2 * width] = low

    def put_halo(ref, u):
        zero = jnp.zeros((group, HALO), BF16)
        for n in range(blocks):
            here = slice(n * group, (n + 1) * group)
            for which in (0, 1):
                first = which * width
                after = before = zero
                if n + 1 < blocks:
                    after = ref[u, (n + 1) * group : (n + 2) * group, first : first + HALO]
                if n:
                    before = ref[u, (n - 1) * group : n * group, first + width - HALO : first + width]
                halo = jnp.where(halo_lane < HALO // 2, after, before)
                if which == 0:
                    again = (halo_lane >= EDGE) & (halo_lane < 3 * EDGE)
                    halo = jnp.where(again, pltpu.roll(halo, 2 * EDGE, 1), halo)
                ref[u, here, 2 * width + which * HALO : 2 * width + (which + 1) * HALO] = halo

    def frame_blur(ref, members, matrix):
        lhs = []
        for u in members:
            center, rest = ref[u, :, 0 : 2 * width], ref[u, :, 2 * width : 2 * width + 2 * HALO]
            lhs.append(jnp.concatenate([center, center[:, 0:width], rest], axis=1))
        out = jnp.dot(jnp.concatenate(lhs, axis=0), matrix, preferred_element_type=F32)
        return {
            u: [out[(k * blocks + n) * group : (k * blocks + n + 1) * group] for n in range(blocks)]
            for k, u in enumerate(members)
        }

    def total8(parts):
        acc = None
        for part in parts:
            for half in range(halves):
                piece = part[:, half * LANES : (half + 1) * LANES].reshape(group // 8, 8, LANES).sum(axis=0)
                acc = piece if acc is None else acc + piece
        rows_sum = jnp.sum(acc, axis=1, keepdims=True)
        zero = jnp.zeros_like(rows_sum)
        upper = jnp.sum(jnp.where(row8 < 4, rows_sum, zero), axis=0, keepdims=True)
        lower = jnp.sum(jnp.where(row8 < 4, zero, rows_sum), axis=0, keepdims=True)
        return upper, lower

    def gather(u, pair):
        for run in range(blocks * halves):
            n, half = run // halves, run % halves
            for mob in range(mobs):
                tiles = [p_ref[at(pair, run, y, mob, rows), :] for y in range(per_lane)]
                for j, tile in enumerate(swap_blocks(tiles, lane, frames)):
                    b = mob * per_lane + j
                    obs_ref[u, n, b * 8 : b * 8 + 8, half * LANES : (half + 1) * LANES] = tile

    def scatter(u, pair):
        for run in range(blocks * halves):
            n, half = run // halves, run % halves
            for mob in range(mobs):
                tiles = []
                for j in range(per_lane):
                    b = mob * per_lane + j
                    tiles.append(est_ref[u, n, b * 8 : b * 8 + 8, half * LANES : (half + 1) * LANES])
                for y, tile in enumerate(swap_blocks(tiles, lane, frames)):
                    out_ref[at(pair, run, y, mob, out_rows), :] = tile

    def forward(u, iteration):
        estimate = obs_ref if iteration == 0 else est_ref
        for n in range(blocks):
            put(left_ref, u, n, scan_blur(estimate[u, n], sf_ref[...]))
        put_halo(left_ref, u)

    def ratios(u, done):
        for n, blurred in enumerate(done[u]):
            put(back_ref, u, n, obs_ref[u, n] / blurred)
        put_halo(back_ref, u)

    def adjoint(u, iteration, done):
        estimate = obs_ref if iteration == 0 else est_ref
        for n, blurred in enumerate(done[u]):
            est_ref[u, n] = estimate[u, n] * scan_blur(blurred, sa_ref[...])

    def statistics(u, pair):
        upper, lower = total8([est_ref[u, n] for n in range(blocks)])
        upper_mean, lower_mean = upper / cells, lower / cells
        mean8 = jnp.where(row8 < 4, upper_mean, lower_mean)
        squares = []
        for n in range(blocks):
            centered = est_ref[u, n].reshape(group // 8, 8, width) - mean8[None]
            centered = centered.astype(BF16).astype(F32).reshape(group, width)
            squares.append(centered * centered)
        upper_sq, lower_sq = total8(squares)
        upper_inv = 1.0 / jnp.sqrt(upper_sq + 1e-06)
        lower_inv = 1.0 / jnp.sqrt(lower_sq + 1e-06)
        held = mean_ref[...]
        held = jnp.where(lane == 2 * pair, upper_mean, held)
        held = jnp.where(lane == 2 * pair + 1, lower_mean, held)
        held = jnp.where(lane == LANES // 2 + 2 * pair, upper_inv, held)
        held = jnp.where(lane == LANES // 2 + 2 * pair + 1, lower_inv, held)
        mean_ref[...] = held

    members = range(units)
    sets = [members[first : first + TOGETHER] for first in range(0, units, TOGETHER)]
    mean_ref[...] = jnp.zeros_like(mean_ref)
    for u in members:
        gather(u, u)
    for copy in copies:
        copy.wait()
    for iteration in range(ITERS):
        for u in members:
            forward(u, iteration)
        for some in sets:
            done = frame_blur(left_ref, some, wf_ref[...])
            for u in some:
                ratios(u, done)
        for some in sets:
            done = frame_blur(back_ref, some, wa_ref[...])
            for u in some:
                adjoint(u, iteration, done)
    for u in members:
        statistics(u, u)
        scatter(u, u)
    for owner in range(owners):
        out_ref[owner * out_rows + rows : (owner + 1) * out_rows, :] = mean_ref[0:STATS, :]


def cross_kernel(q_ref, cross_hbm, centered_ref, cross_ref, out_sem, *, quads):
    owners = LANES
    stride = q_ref.shape[0] // owners
    channels = centered_ref.shape[0]
    tiles = channels // LANES
    column_shards, row_shards, shard_rows, wide = cross_ref.shape
    copies = []
    stats = q_ref[pl.ds(tiles * quads, owners, stride=stride), :]
    stats_t = stats.T
    for k in range(tiles):
        mean = jnp.broadcast_to(stats[:, k : k + 1], (owners, LANES))
        for q in range(quads):
            block = q_ref[pl.ds(k * quads + q, owners, stride=stride), :]
            centered_ref[k * LANES : (k + 1) * LANES, q * LANES : (q + 1) * LANES] = (block - mean).astype(BF16)
    row = jnp.concatenate([stats[:, LANES // 2 + k : LANES // 2 + k + 1] for k in range(PREC // LANES)], axis=0)
    for m in range(column_shards):
        cross = lax.dot_general(
            centered_ref[:PREC, :],
            centered_ref[PREC + m * wide : PREC + (m + 1) * wide, :],
            (((1,), (1,)), ((), ())),
            preferred_element_type=F32,
        )
        first = LANES // 2 + (PREC + m * wide) // LANES
        column = jnp.concatenate([stats_t[first + i : first + i + 1] for i in range(wide // LANES)], axis=1)
        cross_ref[m] = (cross * row * column).reshape(row_shards, shard_rows, wide)
        copies.append(pltpu.make_async_copy(cross_ref.at[m], cross_hbm.at[:, m], out_sem.at[m]))
        copies[-1].start()
    for copy in copies:
        copy.wait()


def finish_kernel(sums_ref, mask_ref, out_ref):
    out_ref[...] = mask_ref[...] * jnp.sum(sums_ref[...], axis=0)


def unpack_kernel(q_ref, est_ref, *, frames, scans):
    owners = LANES
    stride = q_ref.shape[0] // owners
    per_lane = LANES // frames
    quads = scans // per_lane
    tiles = est_ref.shape[0] // (frames * scans)

    def body(k, carry):
        for q in range(quads):
            block = q_ref[pl.ds(k * quads + q, owners, stride=stride), :].T
            for j in range(per_lane):
                est_ref[frame_rows(q * per_lane + j, k, frames, scans, tiles), :] = block[j * frames : (j + 1) * frames]
        return carry

    lax.fori_loop(0, tiles, body, 0)


def local(observed, frame_kernel, scan_kernel, prec_window, frag_window):
    frames, scans, channels = observed.shape
    row_shards, mobs = lax.axis_size("rt"), lax.axis_size("mob")
    owners = row_shards * mobs
    per_lane = LANES // frames
    quads = scans // per_lane
    rows = channels // owners * quads
    group = 8 * per_lane * mobs
    blocks = row_shards * frames // BLOCK
    out_rows = rows + STATS
    width = (channels - PREC) // mobs
    vmem = pl.BlockSpec(memory_space=pltpu.VMEM)
    smem = pl.BlockSpec(memory_space=pltpu.SMEM)
    depth = 3 * BLOCK + 2 * HALO

    hbm = pl.BlockSpec(memory_space=pltpu.HBM)

    def call(kernel, name, out_shape, specs, scratch=(), out_spec=vmem, mib=16.0, micros=5, **statics):
        return pl.pallas_call(
            functools.partial(kernel, **statics),
            out_shape=out_shape,
            in_specs=specs,
            out_specs=jax.tree.map(lambda _: out_spec, out_shape),
            scratch_shapes=scratch,
            compiler_params=pltpu.CompilerParams(vmem_limit_bytes=int(mib * 2**20)),
            cost_estimate=pl.CostEstimate(
                flops=micros * 10**9, bytes_accessed=micros * 3 * 10**6, transcendentals=0
            ),
            name=name,
        )

    shape = jax.ShapeDtypeStruct
    cells = frames * scans
    tiles = channels // LANES
    packed = call(
        pack_kernel,
        "pack",
        shape((owners, rows, LANES), F32),
        [hbm],
        [
            pltpu.VMEM((tiles, cells // 8, 8, LANES), F32),
            pltpu.VMEM((owners * rows, LANES), F32),
            pltpu.SemaphoreType.DMA((tiles,)),
            pltpu.SemaphoreType.DMA((rows // 8,)),
        ],
        out_spec=hbm,
        mib=62,
        frames=frames,
        scans=scans,
    )(to_tiles(observed))
    bands = call(
        bands_kernel,
        "bands",
        (shape((depth, BLOCK), BF16),) * 2 + (shape((2 * group, 2 * group), BF16),) * 2,
        [smem, smem],
        mib=16,
        scans=scans,
        per_lane=per_lane,
    )(frame_kernel, scan_kernel)
    arrived = lax.all_to_all(packed, AXES, 0, 0, tiled=True)
    deblurred = call(
        deblur_kernel,
        "deblur",
        shape((owners * out_rows, LANES), F32),
        [vmem] + [hbm] * 4,
        [pltpu.VMEM(band.shape, BF16) for band in bands]
        + [
            pltpu.VMEM((rows // 8, blocks, group, BLOCK), F32),
            pltpu.VMEM((rows // 8, blocks, group, BLOCK), F32),
            pltpu.VMEM((rows // 8, blocks * group, 2 * BLOCK + 2 * HALO), BF16),
            pltpu.VMEM((rows // 8, blocks * group, 2 * BLOCK + 2 * HALO), BF16),
            pltpu.VMEM((8, LANES), F32),
            pltpu.SemaphoreType.DMA((len(bands),)),
        ],
        mib=40,
        frames=frames,
        mobs=mobs,
        rows=rows,
        cells=cells * owners,
    )(arrived.reshape(owners * rows, LANES), *bands)
    returned = lax.all_to_all(
        deblurred.reshape(owners, out_rows // STATS, STATS, LANES), AXES, 0, 0, tiled=True
    ).reshape(owners * out_rows, LANES)
    cross = call(
        cross_kernel,
        "cross",
        shape((row_shards, mobs, PREC // row_shards, width), F32),
        [vmem],
        [
            pltpu.VMEM((channels, cells), BF16),
            pltpu.VMEM((mobs, row_shards, PREC // row_shards, width), F32),
            pltpu.SemaphoreType.DMA((mobs,)),
        ],
        out_spec=hbm,
        mib=16,
        quads=quads,
    )(returned)
    sums = lax.all_to_all(cross.reshape(owners, PREC // row_shards, width), AXES, 0, 0, tiled=True)
    estimate = call(
        unpack_kernel, "unpack", shape((cells * channels // LANES, LANES), F32), [vmem], frames=frames, scans=scans
    )(returned)
    pair_mask = (prec_window[:, None] == frag_window[None, :]).astype(F32)
    correlation = call(finish_kernel, "finish", shape(pair_mask.shape, F32), [vmem] * 2)(sums, pair_mask)
    return from_tiles(estimate, frames, scans), correlation


def solution(mesh):
    placed = (P("rt", "mob", None), P(), P(), P("rt"), P("mob"))
    return jax.shard_map(
        local,
        mesh=mesh,
        in_specs=placed,
        out_specs=(P("rt", "mob", None), P("rt", "mob")),
        check_vma=False,
    )
```

```python
import functools

import jax
import jax.numpy as jnp
from jax import lax
from jax.experimental import pallas as pl
from jax.experimental.pallas import tpu as pltpu
from jax.sharding import PartitionSpec as P

PREC = 256
ITERS = 2
LANES = 128
AXES = ("rt", "mob")
BLOCK = 256
EDGE = 16
TOGETHER = 2
STATS = 2
HALO = 128

F32 = jnp.float32
BF16 = jnp.bfloat16


def split(values):
    high = values.astype(BF16)
    return high, (values - high.astype(F32)).astype(BF16)


def taps_at(offset, taps_ref, count):
    out = jnp.zeros(offset.shape, F32)
    for tap in range(count):
        out = jnp.where(offset == tap, taps_ref[tap], out)
    return out


def frame_rows(scan, k, frames, scans, tiles):
    return pl.ds((scan // 8 * tiles + k) * 8 + scan % 8, frames, stride=scans * tiles)


def to_tiles(field):
    frames, scans, channels = field.shape
    field = field.reshape(frames, scans // 8, 8, channels // LANES, LANES).transpose(0, 1, 3, 2, 4)
    return field.reshape(frames * scans // 8, channels // LANES, 8, LANES)


def from_tiles(rows, frames, scans):
    tiles = rows.shape[0] // (frames * scans)
    field = rows.reshape(frames, scans // 8, tiles, 8, LANES).transpose(0, 1, 3, 2, 4)
    return field.reshape(frames, scans, tiles * LANES)


def pack_kernel(x_hbm, p_hbm, x_ref, p_ref, in_sem, out_sem, *, frames, scans):
    per_lane = LANES // frames
    quads = scans // per_lane
    owners, rows = LANES, p_ref.shape[0] // LANES
    tiles = x_ref.shape[0]
    steps = rows // 8
    each = tiles // steps

    def arrive(k):
        return pltpu.make_async_copy(x_hbm.at[:, k], x_ref.at[k], in_sem.at[k])

    def leave(step):
        here = pl.ds(pl.multiple_of(step * 8, 8), 8)
        return pltpu.make_async_copy(
            p_ref.reshape(owners, rows, LANES).at[:, here], p_hbm.at[:, here], out_sem.at[step]
        )

    for k in range(tiles):
        arrive(k).start()

    def body(step, carry):
        for sub in range(each):
            k = step * each + sub
            arrive(k).wait()
            view = x_ref.at[k].reshape(frames * scans, LANES)
            for q in range(quads):
                block = jnp.concatenate(
                    [view[pl.ds(q * per_lane + j, frames, stride=scans), :] for j in range(per_lane)], axis=0
                )
                p_ref[pl.ds(k * quads + q, owners, stride=rows), :] = block.T
        leave(step).start()
        return carry

    lax.fori_loop(0, steps, body, 0)
    for step in range(steps):
        leave(step).wait()


def bands_kernel(frame_ref, scan_ref, wf_ref, wa_ref, sf_ref, sa_ref, *, scans, per_lane):
    frame_radius, scan_radius = (frame_ref.shape[0] - 1) // 2, (scan_ref.shape[0] - 1) // 2
    quads = scans // per_lane
    group = sf_ref.shape[0] // 2
    source = lax.broadcasted_iota(jnp.int32, (BLOCK, BLOCK), 0)
    target = lax.broadcasted_iota(jnp.int32, (BLOCK, BLOCK), 1)
    edge_row = lax.broadcasted_iota(jnp.int32, (HALO, BLOCK), 0)
    edge = jnp.where(edge_row < HALO // 2, edge_row + BLOCK, edge_row - HALO)
    again = (edge_row >= EDGE) & (edge_row < 3 * EDGE)
    edge_again = jnp.where(edge_row < 2 * EDGE, edge_row - 2 * EDGE, edge_row - 2 * EDGE + BLOCK)
    edge_target = lax.broadcasted_iota(jnp.int32, (HALO, BLOCK), 1)
    for ref, sign in ((wf_ref, 1), (wa_ref, -1)):
        high, low = split(taps_at(sign * (source - target) + frame_radius, frame_ref, 2 * frame_radius + 1))
        edge_high, _ = split(
            taps_at(sign * (edge - edge_target) + frame_radius, frame_ref, 2 * frame_radius + 1)
        )
        _, edge_low = split(
            taps_at(sign * (edge_again - edge_target) + frame_radius, frame_ref, 2 * frame_radius + 1)
        )
        pieces = (high, high, low, jnp.where(again, edge_low, edge_high), edge_high)
        at = 0
        for piece in pieces:
            ref[at : at + piece.shape[0], :] = piece
            at += piece.shape[0]
    row = lax.broadcasted_iota(jnp.int32, (group, group), 0)
    col = lax.broadcasted_iota(jnp.int32, (group, group), 1)

    def place(index):
        tile, inner = index // 8, index % 8
        scan = (tile // per_lane) * scans + (inner % quads) * per_lane + tile % per_lane
        return scan, inner // quads

    row_scan, row_channel = place(row)
    col_scan, col_channel = place(col)
    for ref, sign in ((sf_ref, 1), (sa_ref, -1)):
        matrix = jnp.where(
            row_channel == col_channel,
            taps_at(sign * (col_scan - row_scan) + scan_radius, scan_ref, 2 * scan_radius + 1),
            0.0,
        )
        high, low = split(matrix)
        ref[0:group, 0:group] = high
        ref[0:group, group : 2 * group] = high
        ref[group : 2 * group, 0:group] = low
        ref[group : 2 * group, group : 2 * group] = jnp.zeros_like(low)


def swap_blocks(tiles, lane, width):
    first, second, third, fourth = tiles
    wide = lane < 2 * width
    narrow = (lane % (2 * width)) < width
    pairs = []
    for a, b in ((first, third), (second, fourth)):
        other = pltpu.roll(jnp.where(wide, b, a), 2 * width, 1)
        pairs.append((jnp.where(wide, a, other), jnp.where(wide, other, b)))
    out = []
    for a, b in zip(pairs[0], pairs[1]):
        out.append(jnp.where(narrow, a, pltpu.roll(b, width, 1)))
        out.append(jnp.where(narrow, pltpu.roll(a, LANES - width, 1), b))
    return out


def deblur_kernel(
    p_ref, wf_ref, wa_ref, sf_ref, sa_ref, out_ref, obs_ref, est_ref, left_ref, back_ref, mean_ref, *, frames, mobs, rows, cells
):
    owners = LANES
    out_rows = out_ref.shape[0] // owners
    units, blocks, group, width = obs_ref.shape
    per_lane = LANES // frames
    lane = lax.broadcasted_iota(jnp.int32, (8, LANES), 1)
    row8 = lax.broadcasted_iota(jnp.int32, (8, 1), 0)
    halo_lane = lax.broadcasted_iota(jnp.int32, (group, HALO), 1)
    halves = width // LANES

    def at(pair, run, y, mob, stride):
        start = ((run * per_lane + y) * mobs + mob) * stride + pair * 8
        return pl.ds(start, 8)

    def scan_blur(values, matrix):
        high, low = split(values)
        both = jnp.dot(matrix, jnp.concatenate([high, low], axis=0), preferred_element_type=F32)
        return both[0:group] + both[group : 2 * group]

    def put(ref, u, n, values):
        high, low = split(values)
        ref[u, n * group : (n + 1) * group, 0:width] = high
        ref[u, n * group : (n + 1) * group, width : 2 * width] = low

    def put_halo(ref, u):
        zero = jnp.zeros((group, HALO), BF16)
        for n in range(blocks):
            here = slice(n * group, (n + 1) * group)
            for which in (0, 1):
                first = which * width
                after = before = zero
                if n + 1 < blocks:
                    after = ref[u, (n + 1) * group : (n + 2) * group, first : first + HALO]
                if n:
                    before = ref[u, (n - 1) * group : n * group, first + width - HALO : first + width]
                halo = jnp.where(halo_lane < HALO // 2, after, before)
                if which == 0:
                    again = (halo_lane >= EDGE) & (halo_lane < 3 * EDGE)
                    halo = jnp.where(again, pltpu.roll(halo, 2 * EDGE, 1), halo)
                ref[u, here, 2 * width + which * HALO : 2 * width + (which + 1) * HALO] = halo

    def frame_blur(ref, members, matrix):
        lhs = []
        for u in members:
            center, rest = ref[u, :, 0 : 2 * width], ref[u, :, 2 * width : 2 * width + 2 * HALO]
            lhs.append(jnp.concatenate([center, center[:, 0:width], rest], axis=1))
        out = jnp.dot(jnp.concatenate(lhs, axis=0), matrix, preferred_element_type=F32)
        return {
            u: [out[(k * blocks + n) * group : (k * blocks + n + 1) * group] for n in range(blocks)]
            for k, u in enumerate(members)
        }

    def total8(parts):
        acc = None
        for part in parts:
            for half in range(halves):
                piece = part[:, half * LANES : (half + 1) * LANES].reshape(group // 8, 8, LANES).sum(axis=0)
                acc = piece if acc is None else acc + piece
        rows_sum = jnp.sum(acc, axis=1, keepdims=True)
        zero = jnp.zeros_like(rows_sum)
        upper = jnp.sum(jnp.where(row8 < 4, rows_sum, zero), axis=0, keepdims=True)
        lower = jnp.sum(jnp.where(row8 < 4, zero, rows_sum), axis=0, keepdims=True)
        return upper, lower

    def gather(u, pair):
        for run in range(blocks * halves):
            n, half = run // halves, run % halves
            for mob in range(mobs):
                tiles = [p_ref[at(pair, run, y, mob, rows), :] for y in range(per_lane)]
                for j, tile in enumerate(swap_blocks(tiles, lane, frames)):
                    b = mob * per_lane + j
                    obs_ref[u, n, b * 8 : b * 8 + 8, half * LANES : (half + 1) * LANES] = tile

    def scatter(u, pair):
        for run in range(blocks * halves):
            n, half = run // halves, run % halves
            for mob in range(mobs):
                tiles = []
                for j in range(per_lane):
                    b = mob * per_lane + j
                    tiles.append(est_ref[u, n, b * 8 : b * 8 + 8, half * LANES : (half + 1) * LANES])
                for y, tile in enumerate(swap_blocks(tiles, lane, frames)):
                    out_ref[at(pair, run, y, mob, out_rows), :] = tile

    def forward(u, iteration):
        estimate = obs_ref if iteration == 0 else est_ref
        for n in range(blocks):
            put(left_ref, u, n, scan_blur(estimate[u, n], sf_ref[...]))
        put_halo(left_ref, u)

    def ratios(u, done):
        for n, blurred in enumerate(done[u]):
            put(back_ref, u, n, obs_ref[u, n] / blurred)
        put_halo(back_ref, u)

    def adjoint(u, iteration, done):
        estimate = obs_ref if iteration == 0 else est_ref
        for n, blurred in enumerate(done[u]):
            est_ref[u, n] = estimate[u, n] * scan_blur(blurred, sa_ref[...])

    def statistics(u, pair):
        upper, lower = total8([est_ref[u, n] for n in range(blocks)])
        upper_mean, lower_mean = upper / cells, lower / cells
        mean8 = jnp.where(row8 < 4, upper_mean, lower_mean)
        squares = []
        for n in range(blocks):
            centered = est_ref[u, n].reshape(group // 8, 8, width) - mean8[None]
            centered = centered.astype(BF16).astype(F32).reshape(group, width)
            squares.append(centered * centered)
        upper_sq, lower_sq = total8(squares)
        upper_inv = 1.0 / jnp.sqrt(upper_sq + 1e-06)
        lower_inv = 1.0 / jnp.sqrt(lower_sq + 1e-06)
        held = mean_ref[...]
        held = jnp.where(lane == 2 * pair, upper_mean, held)
        held = jnp.where(lane == 2 * pair + 1, lower_mean, held)
        held = jnp.where(lane == LANES // 2 + 2 * pair, upper_inv, held)
        held = jnp.where(lane == LANES // 2 + 2 * pair + 1, lower_inv, held)
        mean_ref[...] = held

    members = range(units)
    sets = [members[first : first + TOGETHER] for first in range(0, units, TOGETHER)]
    mean_ref[...] = jnp.zeros_like(mean_ref)
    for u in members:
        gather(u, u)
    for iteration in range(ITERS):
        for u in members:
            forward(u, iteration)
        for some in sets:
            done = frame_blur(left_ref, some, wf_ref[...])
            for u in some:
                ratios(u, done)
        for some in sets:
            done = frame_blur(back_ref, some, wa_ref[...])
            for u in some:
                adjoint(u, iteration, done)
    for u in members:
        statistics(u, u)
        scatter(u, u)
    for owner in range(owners):
        out_ref[owner * out_rows + rows : (owner + 1) * out_rows, :] = mean_ref[0:STATS, :]


def cross_kernel(q_ref, cross_ref, centered_ref, *, quads):
    owners = LANES
    stride = q_ref.shape[0] // owners
    channels = centered_ref.shape[0]
    tiles = channels // LANES
    row_shards, column_shards, shard_rows, wide = cross_ref.shape
    stats = q_ref[pl.ds(tiles * quads, owners, stride=stride), :]
    stats_t = stats.T
    for k in range(tiles):
        mean = jnp.broadcast_to(stats[:, k : k + 1], (owners, LANES))
        for q in range(quads):
            block = q_ref[pl.ds(k * quads + q, owners, stride=stride), :]
            centered_ref[k * LANES : (k + 1) * LANES, q * LANES : (q + 1) * LANES] = (block - mean).astype(BF16)
    row = jnp.concatenate([stats[:, LANES // 2 + k : LANES // 2 + k + 1] for k in range(PREC // LANES)], axis=0)
    for m in range(column_shards):
        cross = lax.dot_general(
            centered_ref[:PREC, :],
            centered_ref[PREC + m * wide : PREC + (m + 1) * wide, :],
            (((1,), (1,)), ((), ())),
            preferred_element_type=F32,
        )
        first = LANES // 2 + (PREC + m * wide) // LANES
        column = jnp.concatenate([stats_t[first + i : first + i + 1] for i in range(wide // LANES)], axis=1)
        cross_ref[:, m] = (cross * row * column).reshape(row_shards, shard_rows, wide)


def finish_kernel(sums_ref, mask_ref, out_ref):
    out_ref[...] = mask_ref[...] * jnp.sum(sums_ref[...], axis=0)


def unpack_kernel(q_ref, est_ref, *, frames, scans):
    owners = LANES
    stride = q_ref.shape[0] // owners
    per_lane = LANES // frames
    quads = scans // per_lane
    tiles = est_ref.shape[0] // (frames * scans)

    def body(k, carry):
        for q in range(quads):
            block = q_ref[pl.ds(k * quads + q, owners, stride=stride), :].T
            for j in range(per_lane):
                est_ref[frame_rows(q * per_lane + j, k, frames, scans, tiles), :] = block[j * frames : (j + 1) * frames]
        return carry

    lax.fori_loop(0, tiles, body, 0)


def local(observed, frame_kernel, scan_kernel, prec_window, frag_window):
    frames, scans, channels = observed.shape
    row_shards, mobs = lax.axis_size("rt"), lax.axis_size("mob")
    owners = row_shards * mobs
    per_lane = LANES // frames
    quads = scans // per_lane
    rows = channels // owners * quads
    group = 8 * per_lane * mobs
    blocks = row_shards * frames // BLOCK
    out_rows = rows + STATS
    width = (channels - PREC) // mobs
    vmem = pl.BlockSpec(memory_space=pltpu.VMEM)
    smem = pl.BlockSpec(memory_space=pltpu.SMEM)
    depth = 3 * BLOCK + 2 * HALO

    hbm = pl.BlockSpec(memory_space=pltpu.HBM)

    def call(kernel, name, out_shape, specs, scratch=(), out_spec=vmem, mib=16.0, micros=5, **statics):
        return pl.pallas_call(
            functools.partial(kernel, **statics),
            out_shape=out_shape,
            in_specs=specs,
            out_specs=jax.tree.map(lambda _: out_spec, out_shape),
            scratch_shapes=scratch,
            compiler_params=pltpu.CompilerParams(vmem_limit_bytes=int(mib * 2**20)),
            cost_estimate=pl.CostEstimate(
                flops=micros * 10**9, bytes_accessed=micros * 3 * 10**6, transcendentals=0
            ),
            name=name,
        )

    shape = jax.ShapeDtypeStruct
    cells = frames * scans
    tiles = channels // LANES
    packed = call(
        pack_kernel,
        "pack",
        shape((owners, rows, LANES), F32),
        [hbm],
        [
            pltpu.VMEM((tiles, cells // 8, 8, LANES), F32),
            pltpu.VMEM((owners * rows, LANES), F32),
            pltpu.SemaphoreType.DMA((tiles,)),
            pltpu.SemaphoreType.DMA((rows // 8,)),
        ],
        out_spec=hbm,
        mib=62,
        frames=frames,
        scans=scans,
    )(to_tiles(observed))
    bands = call(
        bands_kernel,
        "bands",
        (shape((depth, BLOCK), BF16),) * 2 + (shape((2 * group, 2 * group), BF16),) * 2,
        [smem, smem],
        mib=16,
        scans=scans,
        per_lane=per_lane,
    )(frame_kernel, scan_kernel)
    arrived = lax.all_to_all(packed, AXES, 0, 0, tiled=True)
    deblurred = call(
        deblur_kernel,
        "deblur",
        shape((owners * out_rows, LANES), F32),
        [vmem] * 5,
        [
            pltpu.VMEM((rows // 8, blocks, group, BLOCK), F32),
            pltpu.VMEM((rows // 8, blocks, group, BLOCK), F32),
            pltpu.VMEM((rows // 8, blocks * group, 2 * BLOCK + 2 * HALO), BF16),
            pltpu.VMEM((rows // 8, blocks * group, 2 * BLOCK + 2 * HALO), BF16),
            pltpu.VMEM((8, LANES), F32),
        ],
        mib=24,
        frames=frames,
        mobs=mobs,
        rows=rows,
        cells=cells * owners,
    )(arrived.reshape(owners * rows, LANES), *bands)
    returned = lax.all_to_all(
        deblurred.reshape(owners, out_rows // STATS, STATS, LANES), AXES, 0, 0, tiled=True
    ).reshape(owners * out_rows, LANES)
    cross = call(
        cross_kernel,
        "cross",
        shape((row_shards, mobs, PREC // row_shards, width), F32),
        [vmem],
        [pltpu.VMEM((channels, cells), BF16)],
        quads=quads,
    )(returned)
    sums = lax.all_to_all(cross.reshape(owners, PREC // row_shards, width), AXES, 0, 0, tiled=True)
    estimate = call(
        unpack_kernel, "unpack", shape((cells * channels // LANES, LANES), F32), [vmem], frames=frames, scans=scans
    )(returned)
    pair_mask = (prec_window[:, None] == frag_window[None, :]).astype(F32)
    correlation = call(finish_kernel, "finish", shape(pair_mask.shape, F32), [vmem] * 2)(sums, pair_mask)
    return from_tiles(estimate, frames, scans), correlation


def solution(mesh):
    placed = (P("rt", "mob", None), P(), P(), P("rt"), P("mob"))
    return jax.shard_map(
        local,
        mesh=mesh,
        in_specs=placed,
        out_specs=(P("rt", "mob", None), P("rt", "mob")),
        check_vma=False,
    )
```

```python
import functools

import jax
import jax.numpy as jnp
from jax import lax
from jax.experimental import pallas as pl
from jax.experimental.pallas import tpu as pltpu
from jax.sharding import PartitionSpec as P

PREC = 256
ITERS = 2
LANES = 128
AXES = ("rt", "mob")
BLOCK = 256
CORES = 2
EDGE = 16
STATS = 1
HALO = 128

F32 = jnp.float32
BF16 = jnp.bfloat16


def split(values):
    high = values.astype(BF16)
    return high, (values - high.astype(F32)).astype(BF16)


def taps_at(offset, taps_ref, count):
    out = jnp.zeros(offset.shape, F32)
    for tap in range(count):
        out = jnp.where(offset == tap, taps_ref[tap], out)
    return out


def frame_rows(scan, k, frames, scans, tiles):
    return pl.ds((scan // 8 * tiles + k) * 8 + scan % 8, frames, stride=scans * tiles)


def to_tiles(field):
    frames, scans, channels = field.shape
    field = field.reshape(frames, scans // 8, 8, channels // LANES, LANES).transpose(0, 1, 3, 2, 4)
    return field.reshape(frames * scans // 8, channels // LANES, 8, LANES)


def from_tiles(rows, frames, scans):
    tiles = rows.shape[0] // (frames * scans)
    field = rows.reshape(frames, scans // 8, tiles, 8, LANES).transpose(0, 1, 3, 2, 4)
    return field.reshape(frames, scans, tiles * LANES)


def pack_kernel(x_hbm, p_hbm, x_ref, p_ref, in_sem, out_sem, *, frames, scans):
    per_lane = LANES // frames
    quads = scans // per_lane
    owners, rows = LANES, p_ref.shape[0] // LANES
    tiles = x_ref.shape[0]
    steps = rows // 8
    each = tiles // steps

    def arrive(k):
        return pltpu.make_async_copy(x_hbm.at[:, k], x_ref.at[k], in_sem.at[k])

    def leave(step):
        here = pl.ds(pl.multiple_of(step * 8, 8), 8)
        return pltpu.make_async_copy(
            p_ref.reshape(owners, rows, LANES).at[:, here], p_hbm.at[:, here], out_sem.at[step]
        )

    for k in range(tiles):
        arrive(k).start()

    def body(step, carry):
        for sub in range(each):
            k = step * each + sub
            arrive(k).wait()
            view = x_ref.at[k].reshape(frames * scans, LANES)
            for q in range(quads):
                block = jnp.concatenate(
                    [view[pl.ds(q * per_lane + j, frames, stride=scans), :] for j in range(per_lane)], axis=0
                )
                p_ref[pl.ds(k * quads + q, owners, stride=rows), :] = block.T
        leave(step).start()
        return carry

    lax.fori_loop(0, steps, body, 0)
    for step in range(steps):
        leave(step).wait()


def bands_kernel(frame_ref, scan_ref, wf_ref, wa_ref, sf_ref, sa_ref, *, scans, per_lane):
    frame_radius, scan_radius = (frame_ref.shape[0] - 1) // 2, (scan_ref.shape[0] - 1) // 2
    quads = scans // per_lane
    group = sf_ref.shape[0] // 2
    source = lax.broadcasted_iota(jnp.int32, (BLOCK, BLOCK), 0)
    target = lax.broadcasted_iota(jnp.int32, (BLOCK, BLOCK), 1)
    edge_row = lax.broadcasted_iota(jnp.int32, (HALO, BLOCK), 0)
    edge = jnp.where(edge_row < HALO // 2, edge_row + BLOCK, edge_row - HALO)
    again = (edge_row >= EDGE) & (edge_row < 3 * EDGE)
    edge_again = jnp.where(edge_row < 2 * EDGE, edge_row - 2 * EDGE, edge_row - 2 * EDGE + BLOCK)
    edge_target = lax.broadcasted_iota(jnp.int32, (HALO, BLOCK), 1)
    for ref, sign in ((wf_ref, 1), (wa_ref, -1)):
        high, low = split(taps_at(sign * (source - target) + frame_radius, frame_ref, 2 * frame_radius + 1))
        edge_high, _ = split(
            taps_at(sign * (edge - edge_target) + frame_radius, frame_ref, 2 * frame_radius + 1)
        )
        _, edge_low = split(
            taps_at(sign * (edge_again - edge_target) + frame_radius, frame_ref, 2 * frame_radius + 1)
        )
        pieces = (high, high, low, jnp.where(again, edge_low, edge_high), edge_high)
        at = 0
        for piece in pieces:
            ref[at : at + piece.shape[0], :] = piece
            at += piece.shape[0]
    row = lax.broadcasted_iota(jnp.int32, (group, group), 0)
    col = lax.broadcasted_iota(jnp.int32, (group, group), 1)

    def place(index):
        tile, inner = index // 8, index % 8
        scan = (tile // per_lane) * scans + (inner % quads) * per_lane + tile % per_lane
        return scan, inner // quads

    row_scan, row_channel = place(row)
    col_scan, col_channel = place(col)
    for ref, sign in ((sf_ref, 1), (sa_ref, -1)):
        matrix = jnp.where(
            row_channel == col_channel,
            taps_at(sign * (col_scan - row_scan) + scan_radius, scan_ref, 2 * scan_radius + 1),
            0.0,
        )
        high, low = split(matrix)
        ref[0:group, 0:group] = high
        ref[0:group, group : 2 * group] = high
        ref[group : 2 * group, 0:group] = low
        ref[group : 2 * group, group : 2 * group] = jnp.zeros_like(low)


def swap_blocks(tiles, lane, width):
    first, second, third, fourth = tiles
    wide = lane < 2 * width
    narrow = (lane % (2 * width)) < width
    pairs = []
    for a, b in ((first, third), (second, fourth)):
        other = pltpu.roll(jnp.where(wide, b, a), 2 * width, 1)
        pairs.append((jnp.where(wide, a, other), jnp.where(wide, other, b)))
    out = []
    for a, b in zip(pairs[0], pairs[1]):
        out.append(jnp.where(narrow, a, pltpu.roll(b, width, 1)))
        out.append(jnp.where(narrow, pltpu.roll(a, LANES - width, 1), b))
    return out


def deblur_kernel(
    p_ref, wf_ref, wa_ref, sf_ref, sa_ref, out_ref, obs_ref, est_ref, left_ref, back_ref, mean_ref, *, frames, mobs, rows, cells
):
    owners = LANES
    out_rows = out_ref.shape[0] // owners
    units, blocks, group, width = obs_ref.shape
    per_lane = LANES // frames
    lane = lax.broadcasted_iota(jnp.int32, (8, LANES), 1)
    row8 = lax.broadcasted_iota(jnp.int32, (8, 1), 0)
    halo_lane = lax.broadcasted_iota(jnp.int32, (group, HALO), 1)
    halves = width // LANES

    def at(pair, run, y, mob, stride):
        start = ((run * per_lane + y) * mobs + mob) * stride + pair * 8
        return pl.ds(start, 8)

    def scan_blur(values, matrix):
        high, low = split(values)
        return scan_product(matrix, jnp.concatenate([high, low], axis=0))

    def scan_product(matrix, both):
        out = jnp.dot(matrix, both, preferred_element_type=F32)
        return out[0:group] + out[group : 2 * group]

    def put(ref, u, n, values):
        high, low = split(values)
        ref[u, n * group : (n + 1) * group, 0:width] = high
        ref[u, n * group : (n + 1) * group, width : 2 * width] = low

    def put_halo(ref, u):
        zero = jnp.zeros((group, HALO), BF16)
        for n in range(blocks):
            here = slice(n * group, (n + 1) * group)
            for which in (0, 1):
                first = which * width
                after = before = zero
                if n + 1 < blocks:
                    after = ref[u, (n + 1) * group : (n + 2) * group, first : first + HALO]
                if n:
                    before = ref[u, (n - 1) * group : n * group, first + width - HALO : first + width]
                halo = jnp.where(halo_lane < HALO // 2, after, before)
                if which == 0:
                    again = (halo_lane >= EDGE) & (halo_lane < 3 * EDGE)
                    halo = jnp.where(again, pltpu.roll(halo, 2 * EDGE, 1), halo)
                ref[u, here, 2 * width + which * HALO : 2 * width + (which + 1) * HALO] = halo

    def frame_blur(ref, chunks, matrix):
        lhs = []
        for u, first, count in chunks:
            here = slice(first * group, (first + count) * group)
            center, rest = ref[u, here, 0 : 2 * width], ref[u, here, 2 * width : 2 * width + 2 * HALO]
            lhs.append(jnp.concatenate([center, center[:, 0:width], rest], axis=1))
        out = jnp.dot(jnp.concatenate(lhs, axis=0), matrix, preferred_element_type=F32)
        places = [(u, first + n) for u, first, count in chunks for n in range(count)]
        return [(u, n, out[i * group : (i + 1) * group]) for i, (u, n) in enumerate(places)]

    def total8(parts):
        acc = None
        for part in parts:
            for half in range(halves):
                piece = part[:, half * LANES : (half + 1) * LANES].reshape(group // 8, 8, LANES).sum(axis=0)
                acc = piece if acc is None else acc + piece
        rows_sum = jnp.sum(acc, axis=1, keepdims=True)
        zero = jnp.zeros_like(rows_sum)
        upper = jnp.sum(jnp.where(row8 < 4, rows_sum, zero), axis=0, keepdims=True)
        lower = jnp.sum(jnp.where(row8 < 4, zero, rows_sum), axis=0, keepdims=True)
        return upper, lower

    def gather(u, pair):
        for run in range(blocks * halves):
            n, half = run // halves, run % halves
            for mob in range(mobs):
                tiles = [p_ref[at(pair, run, y, mob, rows), :] for y in range(per_lane)]
                for j, tile in enumerate(swap_blocks(tiles, lane, frames)):
                    b = mob * per_lane + j
                    obs_ref[u, n, b * 8 : b * 8 + 8, half * LANES : (half + 1) * LANES] = tile

    def scatter(u, pair):
        for run in range(blocks * halves):
            n, half = run // halves, run % halves
            for mob in range(mobs):
                tiles = []
                for j in range(per_lane):
                    b = mob * per_lane + j
                    tiles.append(est_ref[u, n, b * 8 : b * 8 + 8, half * LANES : (half + 1) * LANES])
                for y, tile in enumerate(swap_blocks(tiles, lane, frames)):
                    out_ref[at(pair, run, y, mob, out_rows), :] = tile

    def forward(u, iteration):
        estimate = obs_ref if iteration == 0 else est_ref
        for n in range(blocks):
            put(left_ref, u, n, scan_blur(estimate[u, n], sf_ref[...]))
        put_halo(left_ref, u)

    def ratios(chunks):
        for u, n, blurred in frame_blur(left_ref, chunks, wf_ref[...]):
            put(back_ref, u, n, obs_ref[u, n] / blurred)

    def adjoint_frames(chunks):
        for u, n, blurred in frame_blur(back_ref, chunks, wa_ref[...]):
            put(left_ref, u, n, blurred)

    def adjoint_scans(u, iteration):
        estimate = obs_ref if iteration == 0 else est_ref
        for n in range(blocks):
            here = slice(n * group, (n + 1) * group)
            both = jnp.concatenate([left_ref[u, here, 0:width], left_ref[u, here, width : 2 * width]], axis=0)
            est_ref[u, n] = estimate[u, n] * scan_product(sa_ref[...], both)

    def statistics(u, pair):
        upper, lower = total8([est_ref[u, n] for n in range(blocks)])
        upper_mean, lower_mean = upper / cells, lower / cells
        mean8 = jnp.where(row8 < 4, upper_mean, lower_mean)
        squares = []
        for n in range(blocks):
            centered = est_ref[u, n].reshape(group // 8, 8, width) - mean8[None]
            centered = centered.astype(BF16).astype(F32).reshape(group, width)
            squares.append(centered * centered)
        upper_sq, lower_sq = total8(squares)
        upper_inv = 1.0 / jnp.sqrt(upper_sq + 1e-06)
        lower_inv = 1.0 / jnp.sqrt(lower_sq + 1e-06)
        held = mean_ref[...]
        held = jnp.where(lane == 2 * pair, upper_mean, held)
        held = jnp.where(lane == 2 * pair + 1, lower_mean, held)
        held = jnp.where(lane == LANES // 2 + 2 * pair, upper_inv, held)
        held = jnp.where(lane == LANES // 2 + 2 * pair + 1, lower_inv, held)
        mean_ref[...] = held

    members = range(units)
    sets = [[(u, 0, blocks)] for u in members]
    mean_ref[...] = jnp.zeros_like(mean_ref)
    for u in members:
        gather(u, u)
    for iteration in range(ITERS):
        for u in members:
            forward(u, iteration)
        for chunks in sets:
            ratios(chunks)
        for u in members:
            put_halo(back_ref, u)
        for chunks in sets:
            adjoint_frames(chunks)
        for u in members:
            adjoint_scans(u, iteration)
    for u in members:
        statistics(u, u)
        scatter(u, u)
    for owner in range(owners):
        out_ref[owner * out_rows + rows : (owner + 1) * out_rows, :] = mean_ref[0:STATS, :]


def cross_kernel(q_ref, keep_ref, send_ref, centered_ref, *, quads):
    owners = LANES
    stride = q_ref.shape[0] // owners
    core = lax.axis_index("mob") % CORES
    channels = centered_ref.shape[0]
    tiles = channels // LANES
    row_shards, chips, shard_rows, wide = keep_ref.shape
    stats = q_ref[pl.ds(tiles * quads, owners, stride=stride), :]
    stats_t = stats.T
    for k in range(tiles):
        mean = jnp.broadcast_to(stats[:, k : k + 1], (owners, LANES))
        for q in range(quads):
            block = q_ref[pl.ds(k * quads + q, owners, stride=stride), :]
            centered_ref[k * LANES : (k + 1) * LANES, q * LANES : (q + 1) * LANES] = (block - mean).astype(BF16)
    row = jnp.concatenate([stats[:, LANES // 2 + k : LANES // 2 + k + 1] for k in range(PREC // LANES)], axis=0)
    for m in range(chips * CORES):
        cross = lax.dot_general(
            centered_ref[:PREC, :],
            centered_ref[PREC + m * wide : PREC + (m + 1) * wide, :],
            (((1,), (1,)), ((), ())),
            preferred_element_type=F32,
        )
        first = LANES // 2 + (PREC + m * wide) // LANES
        column = jnp.concatenate([stats_t[first + i : first + i + 1] for i in range(wide // LANES)], axis=1)
        cross = (cross * row * column).reshape(row_shards, shard_rows, wide)

        def store(ref, cross=cross, chip=m // CORES):
            ref[:, chip] = cross

        pl.when(core == m % CORES)(functools.partial(store, keep_ref))
        pl.when(core != m % CORES)(functools.partial(store, send_ref))


def finish_kernel(sums_ref, mask_ref, out_ref):
    out_ref[...] = mask_ref[...] * jnp.sum(sums_ref[...], axis=0)


def unpack_kernel(q_ref, est_ref, *, frames, scans):
    owners = LANES
    stride = q_ref.shape[0] // owners
    per_lane = LANES // frames
    quads = scans // per_lane
    tiles = est_ref.shape[0] // (frames * scans)

    def body(k, carry):
        for q in range(quads):
            block = q_ref[pl.ds(k * quads + q, owners, stride=stride), :].T
            for j in range(per_lane):
                est_ref[frame_rows(q * per_lane + j, k, frames, scans, tiles), :] = block[j * frames : (j + 1) * frames]
        return carry

    lax.fori_loop(0, tiles, body, 0)


def local(observed, frame_kernel, scan_kernel, prec_window, frag_window):
    frames, scans, channels = observed.shape
    row_shards, mobs = lax.axis_size("rt"), lax.axis_size("mob")
    owners = row_shards * mobs
    per_lane = LANES // frames
    quads = scans // per_lane
    rows = channels // owners * quads
    group = 8 * per_lane * mobs
    blocks = row_shards * frames // BLOCK
    out_rows = rows + STATS
    width = (channels - PREC) // mobs
    vmem = pl.BlockSpec(memory_space=pltpu.VMEM)
    smem = pl.BlockSpec(memory_space=pltpu.SMEM)
    depth = 3 * BLOCK + 2 * HALO

    hbm = pl.BlockSpec(memory_space=pltpu.HBM)

    def call(kernel, name, out_shape, specs, scratch=(), out_spec=vmem, mib=16.0, micros=5, **statics):
        return pl.pallas_call(
            functools.partial(kernel, **statics),
            out_shape=out_shape,
            in_specs=specs,
            out_specs=jax.tree.map(lambda _: out_spec, out_shape),
            scratch_shapes=scratch,
            compiler_params=pltpu.CompilerParams(vmem_limit_bytes=int(mib * 2**20)),
            cost_estimate=pl.CostEstimate(
                flops=micros * 10**9, bytes_accessed=micros * 3 * 10**6, transcendentals=0
            ),
            name=name,
        )

    shape = jax.ShapeDtypeStruct
    cells = frames * scans
    tiles = channels // LANES
    packed = call(
        pack_kernel,
        "pack",
        shape((owners, rows, LANES), F32),
        [hbm],
        [
            pltpu.VMEM((tiles, cells // 8, 8, LANES), F32),
            pltpu.VMEM((owners * rows, LANES), F32),
            pltpu.SemaphoreType.DMA((tiles,)),
            pltpu.SemaphoreType.DMA((rows // 8,)),
        ],
        out_spec=hbm,
        mib=62,
        frames=frames,
        scans=scans,
    )(to_tiles(observed))
    bands = call(
        bands_kernel,
        "bands",
        (shape((depth, BLOCK), BF16),) * 2 + (shape((2 * group, 2 * group), BF16),) * 2,
        [smem, smem],
        mib=16,
        scans=scans,
        per_lane=per_lane,
    )(frame_kernel, scan_kernel)
    arrived = lax.all_to_all(packed, AXES, 0, 0, tiled=True)
    deblurred = call(
        deblur_kernel,
        "deblur",
        shape((owners * out_rows, LANES), F32),
        [vmem] * 5,
        [
            pltpu.VMEM((rows // 8, blocks, group, BLOCK), F32),
            pltpu.VMEM((rows // 8, blocks, group, BLOCK), F32),
            pltpu.VMEM((rows // 8, blocks * group, 2 * BLOCK + 2 * HALO), BF16),
            pltpu.VMEM((rows // 8, blocks * group, 2 * BLOCK + 2 * HALO), BF16),
            pltpu.VMEM((8, LANES), F32),
        ],
        mib=24,
        frames=frames,
        mobs=mobs,
        rows=rows,
        cells=cells * owners,
    )(arrived.reshape(owners * rows, LANES), *bands)
    returned = lax.all_to_all(
        deblurred.reshape(owners, out_rows // STATS, STATS, LANES), AXES, 0, 0, tiled=True
    ).reshape(owners * out_rows, LANES)
    half = shape((row_shards, mobs // CORES, PREC // row_shards, width), F32)
    keep, send = call(
        cross_kernel, "cross", (half, half), [vmem], [pltpu.VMEM((channels, cells), BF16)], quads=quads
    )(returned)
    both = keep + lax.ppermute(send, "mob", [(m, m ^ 1) for m in range(mobs)])
    groups = [[first + CORES * d for d in range(owners // CORES)] for first in range(CORES)]
    sums = lax.all_to_all(
        both.reshape(owners // CORES, PREC // row_shards, width), AXES, 0, 0, axis_index_groups=groups, tiled=True
    )
    estimate = call(
        unpack_kernel, "unpack", shape((cells * channels // LANES, LANES), F32), [vmem], frames=frames, scans=scans
    )(returned)
    pair_mask = (prec_window[:, None] == frag_window[None, :]).astype(F32)
    correlation = call(finish_kernel, "finish", shape(pair_mask.shape, F32), [vmem] * 2)(sums, pair_mask)
    return from_tiles(estimate, frames, scans), correlation


def solution(mesh):
    placed = (P("rt", "mob", None), P(), P(), P("rt"), P("mob"))
    return jax.shard_map(
        local,
        mesh=mesh,
        in_specs=placed,
        out_specs=(P("rt", "mob", None), P("rt", "mob")),
        check_vma=False,
    )
```

```python
import functools

import jax
import jax.numpy as jnp
from jax import lax
from jax.experimental import pallas as pl
from jax.experimental.pallas import tpu as pltpu
from jax.sharding import PartitionSpec as P

PREC = 256
ITERS = 2
LANES = 128
AXES = ("rt", "mob")
BLOCK = 256
CORES = 2
EDGE = 16
STATS = 1
HALO = 128

F32 = jnp.float32
BF16 = jnp.bfloat16


def split(values):
    high = values.astype(BF16)
    return high, (values - high.astype(F32)).astype(BF16)


def taps_at(offset, taps_ref, count):
    out = jnp.zeros(offset.shape, F32)
    for tap in range(count):
        out = jnp.where(offset == tap, taps_ref[tap], out)
    return out


def frame_rows(scan, k, frames, scans, tiles):
    return pl.ds((scan // 8 * tiles + k) * 8 + scan % 8, frames, stride=scans * tiles)


def to_tiles(field):
    frames, scans, channels = field.shape
    field = field.reshape(frames, scans // 8, 8, channels // LANES, LANES).transpose(0, 1, 3, 2, 4)
    return field.reshape(frames * scans // 8, channels // LANES, 8, LANES)


def from_tiles(rows, frames, scans):
    tiles = rows.shape[0] // (frames * scans)
    field = rows.reshape(frames, scans // 8, tiles, 8, LANES).transpose(0, 1, 3, 2, 4)
    return field.reshape(frames, scans, tiles * LANES)


def pack_kernel(x_hbm, p_hbm, x_ref, p_ref, in_sem, out_sem, *, frames, scans):
    per_lane = LANES // frames
    quads = scans // per_lane
    owners, rows = LANES, p_ref.shape[0] // LANES
    tiles = x_ref.shape[0]
    steps = rows // 8
    each = tiles // steps

    def arrive(k):
        return pltpu.make_async_copy(x_hbm.at[:, k], x_ref.at[k], in_sem.at[k])

    def leave(step):
        here = pl.ds(pl.multiple_of(step * 8, 8), 8)
        return pltpu.make_async_copy(
            p_ref.reshape(owners, rows, LANES).at[:, here], p_hbm.at[:, here], out_sem.at[step]
        )

    for k in range(tiles):
        arrive(k).start()

    def body(step, carry):
        for sub in range(each):
            k = step * each + sub
            arrive(k).wait()
            view = x_ref.at[k].reshape(frames * scans, LANES)
            for q in range(quads):
                block = jnp.concatenate(
                    [view[pl.ds(q * per_lane + j, frames, stride=scans), :] for j in range(per_lane)], axis=0
                )
                p_ref[pl.ds(k * quads + q, owners, stride=rows), :] = block.T
        leave(step).start()
        return carry

    lax.fori_loop(0, steps, body, 0)
    for step in range(steps):
        leave(step).wait()


def bands_kernel(frame_ref, scan_ref, sf_ref, sa_ref, wf_ref, wa_ref, *, scans, per_lane):
    frame_radius, scan_radius = (frame_ref.shape[0] - 1) // 2, (scan_ref.shape[0] - 1) // 2
    quads = scans // per_lane
    group = sf_ref.shape[0] // 2
    source = lax.broadcasted_iota(jnp.int32, (BLOCK, BLOCK), 0)
    target = lax.broadcasted_iota(jnp.int32, (BLOCK, BLOCK), 1)
    edge_row = lax.broadcasted_iota(jnp.int32, (HALO, BLOCK), 0)
    edge = jnp.where(edge_row < HALO // 2, edge_row + BLOCK, edge_row - HALO)
    again = (edge_row >= EDGE) & (edge_row < 3 * EDGE)
    edge_again = jnp.where(edge_row < 2 * EDGE, edge_row - 2 * EDGE, edge_row - 2 * EDGE + BLOCK)
    edge_target = lax.broadcasted_iota(jnp.int32, (HALO, BLOCK), 1)
    for ref, sign in ((wf_ref, 1), (wa_ref, -1)):
        high, low = split(taps_at(sign * (source - target) + frame_radius, frame_ref, 2 * frame_radius + 1))
        edge_high, _ = split(
            taps_at(sign * (edge - edge_target) + frame_radius, frame_ref, 2 * frame_radius + 1)
        )
        _, edge_low = split(
            taps_at(sign * (edge_again - edge_target) + frame_radius, frame_ref, 2 * frame_radius + 1)
        )
        pieces = (high, high, low, jnp.where(again, edge_low, edge_high), edge_high)
        at = 0
        for piece in pieces:
            ref[at : at + piece.shape[0], :] = piece
            at += piece.shape[0]
    row = lax.broadcasted_iota(jnp.int32, (group, group), 0)
    col = lax.broadcasted_iota(jnp.int32, (group, group), 1)

    def place(index):
        tile, inner = index // 8, index % 8
        scan = (tile // per_lane) * scans + (inner % quads) * per_lane + tile % per_lane
        return scan, inner // quads

    row_scan, row_channel = place(row)
    col_scan, col_channel = place(col)
    for ref, sign in ((sf_ref, 1), (sa_ref, -1)):
        matrix = jnp.where(
            row_channel == col_channel,
            taps_at(sign * (col_scan - row_scan) + scan_radius, scan_ref, 2 * scan_radius + 1),
            0.0,
        )
        high, low = split(matrix)
        ref[0:group, 0:group] = high
        ref[0:group, group : 2 * group] = high
        ref[group : 2 * group, 0:group] = low
        ref[group : 2 * group, group : 2 * group] = jnp.zeros_like(low)


def swap_blocks(tiles, lane, width):
    first, second, third, fourth = tiles
    wide = lane < 2 * width
    narrow = (lane % (2 * width)) < width
    pairs = []
    for a, b in ((first, third), (second, fourth)):
        other = pltpu.roll(jnp.where(wide, b, a), 2 * width, 1)
        pairs.append((jnp.where(wide, a, other), jnp.where(wide, other, b)))
    out = []
    for a, b in zip(pairs[0], pairs[1]):
        out.append(jnp.where(narrow, a, pltpu.roll(b, width, 1)))
        out.append(jnp.where(narrow, pltpu.roll(a, LANES - width, 1), b))
    return out


def deblur_kernel(
    p_ref, sf_ref, sa_ref, wf_ref, wa_ref, out_ref, obs_ref, est_ref, left_ref, back_ref, mean_ref, *, frames, mobs, rows, cells
):
    owners = LANES
    out_rows = out_ref.shape[0] // owners
    units, blocks, group, width = obs_ref.shape
    per_lane = LANES // frames
    lane = lax.broadcasted_iota(jnp.int32, (8, LANES), 1)
    row8 = lax.broadcasted_iota(jnp.int32, (8, 1), 0)
    halo_lane = lax.broadcasted_iota(jnp.int32, (group, HALO), 1)
    halves = width // LANES

    def at(pair, run, y, mob, stride):
        start = ((run * per_lane + y) * mobs + mob) * stride + pair * 8
        return pl.ds(start, 8)

    def scan_blur(values, matrix):
        high, low = split(values)
        return scan_product(matrix, jnp.concatenate([high, low], axis=0))

    def scan_product(matrix, both):
        out = jnp.dot(matrix, both, preferred_element_type=F32)
        return out[0:group] + out[group : 2 * group]

    def put(ref, u, n, values):
        high, low = split(values)
        ref[u, n * group : (n + 1) * group, 0:width] = high
        ref[u, n * group : (n + 1) * group, width : 2 * width] = low

    def put_halo(ref, u):
        zero = jnp.zeros((group, HALO), BF16)
        for n in range(blocks):
            here = slice(n * group, (n + 1) * group)
            for which in (0, 1):
                first = which * width
                after = before = zero
                if n + 1 < blocks:
                    after = ref[u, (n + 1) * group : (n + 2) * group, first : first + HALO]
                if n:
                    before = ref[u, (n - 1) * group : n * group, first + width - HALO : first + width]
                halo = jnp.where(halo_lane < HALO // 2, after, before)
                if which == 0:
                    again = (halo_lane >= EDGE) & (halo_lane < 3 * EDGE)
                    halo = jnp.where(again, pltpu.roll(halo, 2 * EDGE, 1), halo)
                ref[u, here, 2 * width + which * HALO : 2 * width + (which + 1) * HALO] = halo

    def frame_blur(ref, chunks, matrix):
        lhs = []
        for u, first, count in chunks:
            here = slice(first * group, (first + count) * group)
            center, rest = ref[u, here, 0 : 2 * width], ref[u, here, 2 * width : 2 * width + 2 * HALO]
            lhs.append(jnp.concatenate([center, center[:, 0:width], rest], axis=1))
        out = jnp.dot(jnp.concatenate(lhs, axis=0), matrix, preferred_element_type=F32)
        places = [(u, first + n) for u, first, count in chunks for n in range(count)]
        return [(u, n, out[i * group : (i + 1) * group]) for i, (u, n) in enumerate(places)]

    def total8(parts):
        acc = None
        for part in parts:
            for half in range(halves):
                piece = part[:, half * LANES : (half + 1) * LANES].reshape(group // 8, 8, LANES).sum(axis=0)
                acc = piece if acc is None else acc + piece
        rows_sum = jnp.sum(acc, axis=1, keepdims=True)
        zero = jnp.zeros_like(rows_sum)
        upper = jnp.sum(jnp.where(row8 < 4, rows_sum, zero), axis=0, keepdims=True)
        lower = jnp.sum(jnp.where(row8 < 4, zero, rows_sum), axis=0, keepdims=True)
        return upper, lower

    def gather(u, pair):
        for run in range(blocks * halves):
            n, half = run // halves, run % halves
            for mob in range(mobs):
                tiles = [p_ref[at(pair, run, y, mob, rows), :] for y in range(per_lane)]
                for j, tile in enumerate(swap_blocks(tiles, lane, frames)):
                    b = mob * per_lane + j
                    obs_ref[u, n, b * 8 : b * 8 + 8, half * LANES : (half + 1) * LANES] = tile

    def scatter(u, pair):
        for run in range(blocks * halves):
            n, half = run // halves, run % halves
            for mob in range(mobs):
                tiles = []
                for j in range(per_lane):
                    b = mob * per_lane + j
                    tiles.append(est_ref[u, n, b * 8 : b * 8 + 8, half * LANES : (half + 1) * LANES])
                for y, tile in enumerate(swap_blocks(tiles, lane, frames)):
                    out_ref[at(pair, run, y, mob, out_rows), :] = tile

    def forward(u, iteration):
        estimate = obs_ref if iteration == 0 else est_ref
        for n in range(blocks):
            put(left_ref, u, n, scan_blur(estimate[u, n], sf_ref[...]))
        put_halo(left_ref, u)

    def ratios(chunks):
        for u, n, blurred in frame_blur(left_ref, chunks, wf_ref[...]):
            put(back_ref, u, n, obs_ref[u, n] / blurred)

    def adjoint_frames(chunks):
        for u, n, blurred in frame_blur(back_ref, chunks, wa_ref[...]):
            put(left_ref, u, n, blurred)

    def adjoint_scans(u, iteration):
        estimate = obs_ref if iteration == 0 else est_ref
        for n in range(blocks):
            here = slice(n * group, (n + 1) * group)
            both = jnp.concatenate([left_ref[u, here, 0:width], left_ref[u, here, width : 2 * width]], axis=0)
            est_ref[u, n] = estimate[u, n] * scan_product(sa_ref[...], both)

    def statistics(u, pair):
        upper, lower = total8([est_ref[u, n] for n in range(blocks)])
        upper_mean, lower_mean = upper / cells, lower / cells
        mean8 = jnp.where(row8 < 4, upper_mean, lower_mean)
        squares = []
        for n in range(blocks):
            centered = est_ref[u, n].reshape(group // 8, 8, width) - mean8[None]
            centered = centered.astype(BF16).astype(F32).reshape(group, width)
            squares.append(centered * centered)
        upper_sq, lower_sq = total8(squares)
        upper_inv = 1.0 / jnp.sqrt(upper_sq + 1e-06)
        lower_inv = 1.0 / jnp.sqrt(lower_sq + 1e-06)
        held = mean_ref[...]
        held = jnp.where(lane == 2 * pair, upper_mean, held)
        held = jnp.where(lane == 2 * pair + 1, lower_mean, held)
        held = jnp.where(lane == LANES // 2 + 2 * pair, upper_inv, held)
        held = jnp.where(lane == LANES // 2 + 2 * pair + 1, lower_inv, held)
        mean_ref[...] = held

    members = range(units)
    sets = [[(u, 0, blocks)] for u in members]
    mean_ref[...] = jnp.zeros_like(mean_ref)
    for u in members:
        gather(u, u)
    for iteration in range(ITERS):
        for u in members:
            forward(u, iteration)
        for chunks in sets:
            ratios(chunks)
        for u in members:
            put_halo(back_ref, u)
        for chunks in sets:
            adjoint_frames(chunks)
        for u in members:
            adjoint_scans(u, iteration)
    for u in members:
        statistics(u, u)
        scatter(u, u)
    for owner in range(owners):
        out_ref[owner * out_rows + rows : (owner + 1) * out_rows, :] = mean_ref[0:STATS, :]


def cross_kernel(q_ref, keep_ref, send_ref, centered_ref, *, quads):
    owners = LANES
    stride = q_ref.shape[0] // owners
    core = lax.axis_index("mob") % CORES
    channels = centered_ref.shape[0]
    tiles = channels // LANES
    row_shards, chips, shard_rows, wide = keep_ref.shape
    stats = q_ref[pl.ds(tiles * quads, owners, stride=stride), :]
    stats_t = stats.T
    for k in range(tiles):
        mean = jnp.broadcast_to(stats[:, k : k + 1], (owners, LANES))
        for q in range(quads):
            block = q_ref[pl.ds(k * quads + q, owners, stride=stride), :]
            centered_ref[k * LANES : (k + 1) * LANES, q * LANES : (q + 1) * LANES] = (block - mean).astype(BF16)
    row = jnp.concatenate([stats[:, LANES // 2 + k : LANES // 2 + k + 1] for k in range(PREC // LANES)], axis=0)

    def product(m):
        cross = lax.dot_general(
            centered_ref[:PREC, :],
            centered_ref[PREC + m * wide : PREC + (m + 1) * wide, :],
            (((1,), (1,)), ((), ())),
            preferred_element_type=F32,
        )
        first = LANES // 2 + (PREC + m * wide) // LANES
        column = jnp.concatenate([stats_t[first + i : first + i + 1] for i in range(wide // LANES)], axis=1)
        return (cross * row * column).reshape(row_shards, shard_rows, wide)

    for chip in range(chips):
        even, odd = product(chip * CORES), product(chip * CORES + 1)
        keep_ref[:, chip] = jnp.where(core == 0, even, odd)
        send_ref[:, chip] = jnp.where(core == 0, odd, even)


def finish_kernel(sums_ref, mask_ref, out_ref):
    out_ref[...] = mask_ref[...] * jnp.sum(sums_ref[...], axis=0)


def unpack_kernel(q_ref, est_ref, *, frames, scans):
    owners = LANES
    stride = q_ref.shape[0] // owners
    per_lane = LANES // frames
    quads = scans // per_lane
    tiles = est_ref.shape[0] // (frames * scans)

    def body(k, carry):
        for q in range(quads):
            block = q_ref[pl.ds(k * quads + q, owners, stride=stride), :].T
            for j in range(per_lane):
                est_ref[frame_rows(q * per_lane + j, k, frames, scans, tiles), :] = block[j * frames : (j + 1) * frames]
        return carry

    lax.fori_loop(0, tiles, body, 0)


def local(observed, frame_kernel, scan_kernel, prec_window, frag_window):
    frames, scans, channels = observed.shape
    row_shards, mobs = lax.axis_size("rt"), lax.axis_size("mob")
    owners = row_shards * mobs
    per_lane = LANES // frames
    quads = scans // per_lane
    rows = channels // owners * quads
    group = 8 * per_lane * mobs
    blocks = row_shards * frames // BLOCK
    out_rows = rows + STATS
    width = (channels - PREC) // mobs
    vmem = pl.BlockSpec(memory_space=pltpu.VMEM)
    smem = pl.BlockSpec(memory_space=pltpu.SMEM)
    depth = 3 * BLOCK + 2 * HALO

    hbm = pl.BlockSpec(memory_space=pltpu.HBM)

    def call(kernel, name, out_shape, specs, scratch=(), out_spec=vmem, mib=16.0, micros=5, **statics):
        return pl.pallas_call(
            functools.partial(kernel, **statics),
            out_shape=out_shape,
            in_specs=specs,
            out_specs=jax.tree.map(lambda _: out_spec, out_shape),
            scratch_shapes=scratch,
            compiler_params=pltpu.CompilerParams(vmem_limit_bytes=int(mib * 2**20)),
            cost_estimate=pl.CostEstimate(
                flops=micros * 10**9, bytes_accessed=micros * 3 * 10**6, transcendentals=0
            ),
            name=name,
        )

    shape = jax.ShapeDtypeStruct
    cells = frames * scans
    tiles = channels // LANES
    packed = call(
        pack_kernel,
        "pack",
        shape((owners, rows, LANES), F32),
        [hbm],
        [
            pltpu.VMEM((tiles, cells // 8, 8, LANES), F32),
            pltpu.VMEM((owners * rows, LANES), F32),
            pltpu.SemaphoreType.DMA((tiles,)),
            pltpu.SemaphoreType.DMA((rows // 8,)),
        ],
        out_spec=hbm,
        mib=62,
        frames=frames,
        scans=scans,
    )(to_tiles(observed))
    bands = call(
        bands_kernel,
        "bands",
        (shape((2 * group, 2 * group), BF16),) * 2 + (shape((depth, BLOCK), BF16),) * 2,
        [smem, smem],
        mib=16,
        scans=scans,
        per_lane=per_lane,
    )(frame_kernel, scan_kernel)
    arrived = lax.all_to_all(packed, AXES, 0, 0, tiled=True)
    deblurred = call(
        deblur_kernel,
        "deblur",
        shape((owners * out_rows, LANES), F32),
        [vmem] * 5,
        [
            pltpu.VMEM((rows // 8, blocks, group, BLOCK), F32),
            pltpu.VMEM((rows // 8, blocks, group, BLOCK), F32),
            pltpu.VMEM((rows // 8, blocks * group, 2 * BLOCK + 2 * HALO), BF16),
            pltpu.VMEM((rows // 8, blocks * group, 2 * BLOCK + 2 * HALO), BF16),
            pltpu.VMEM((8, LANES), F32),
        ],
        mib=18,
        frames=frames,
        mobs=mobs,
        rows=rows,
        cells=cells * owners,
    )(arrived.reshape(owners * rows, LANES), *bands)
    returned = lax.all_to_all(
        deblurred.reshape(owners, out_rows // STATS, STATS, LANES), AXES, 0, 0, tiled=True
    ).reshape(owners * out_rows, LANES)
    half = shape((row_shards, mobs // CORES, PREC // row_shards, width), F32)
    keep, send = call(
        cross_kernel, "cross", (half, half), [vmem], [pltpu.VMEM((channels, cells), BF16)], quads=quads
    )(returned)
    both = keep + lax.ppermute(send, "mob", [(m, m ^ 1) for m in range(mobs)])
    groups = [[first + CORES * d for d in range(owners // CORES)] for first in range(CORES)]
    sums = lax.all_to_all(
        both.reshape(owners // CORES, PREC // row_shards, width), AXES, 0, 0, axis_index_groups=groups, tiled=True
    )
    estimate = call(
        unpack_kernel, "unpack", shape((cells * channels // LANES, LANES), F32), [vmem], frames=frames, scans=scans
    )(returned)
    pair_mask = (prec_window[:, None] == frag_window[None, :]).astype(F32)
    correlation = call(finish_kernel, "finish", shape(pair_mask.shape, F32), [vmem] * 2)(sums, pair_mask)
    return from_tiles(estimate, frames, scans), correlation


def solution(mesh):
    placed = (P("rt", "mob", None), P(), P(), P("rt"), P("mob"))
    return jax.shard_map(
        local,
        mesh=mesh,
        in_specs=placed,
        out_specs=(P("rt", "mob", None), P("rt", "mob")),
        check_vma=False,
    )
```

```python
import functools

import jax
import jax.numpy as jnp
from jax import lax
from jax.experimental import pallas as pl
from jax.experimental.pallas import tpu as pltpu
from jax.sharding import PartitionSpec as P

PREC = 256
ITERS = 2
LANES = 128
AXES = ("rt", "mob")
BLOCK = 256
CORES = 2
EDGE = 16
STATS = 1
HALO = 128

F32 = jnp.float32
BF16 = jnp.bfloat16


def split(values):
    high = values.astype(BF16)
    return high, (values - high.astype(F32)).astype(BF16)


def taps_at(offset, taps_ref, count):
    out = jnp.zeros(offset.shape, F32)
    for tap in range(count):
        out = jnp.where(offset == tap, taps_ref[tap], out)
    return out


def frame_rows(scan, k, frames, scans, tiles):
    return pl.ds((scan // 8 * tiles + k) * 8 + scan % 8, frames, stride=scans * tiles)


def to_tiles(field):
    frames, scans, channels = field.shape
    field = field.reshape(frames, scans // 8, 8, channels // LANES, LANES).transpose(0, 1, 3, 2, 4)
    return field.reshape(frames * scans // 8, channels // LANES, 8, LANES)


def from_tiles(rows, frames, scans):
    tiles = rows.shape[0] // (frames * scans)
    field = rows.reshape(frames, scans // 8, tiles, 8, LANES).transpose(0, 1, 3, 2, 4)
    return field.reshape(frames, scans, tiles * LANES)


def pack_kernel(x_hbm, p_hbm, x_ref, p_ref, in_sem, out_sem, *, frames, scans):
    per_lane = LANES // frames
    quads = scans // per_lane
    owners, rows = LANES, p_ref.shape[0] // LANES
    tiles = x_ref.shape[0]
    steps = rows // 8
    each = tiles // steps

    def arrive(k):
        return pltpu.make_async_copy(x_hbm.at[:, k], x_ref.at[k], in_sem.at[k])

    def leave(step):
        here = pl.ds(pl.multiple_of(step * 8, 8), 8)
        return pltpu.make_async_copy(
            p_ref.reshape(owners, rows, LANES).at[:, here], p_hbm.at[:, here], out_sem.at[step]
        )

    for k in range(tiles):
        arrive(k).start()

    def body(step, carry):
        for sub in range(each):
            k = step * each + sub
            arrive(k).wait()
            view = x_ref.at[k].reshape(frames * scans, LANES)
            for q in range(quads):
                block = jnp.concatenate(
                    [view[pl.ds(q * per_lane + j, frames, stride=scans), :] for j in range(per_lane)], axis=0
                )
                p_ref[pl.ds(k * quads + q, owners, stride=rows), :] = block.T
        leave(step).start()
        return carry

    lax.fori_loop(0, steps, body, 0)
    for step in range(steps):
        leave(step).wait()


def bands_kernel(frame_ref, scan_ref, sf_ref, sa_ref, wf_ref, wa_ref, *, scans, per_lane):
    frame_radius, scan_radius = (frame_ref.shape[0] - 1) // 2, (scan_ref.shape[0] - 1) // 2
    quads = scans // per_lane
    group = sf_ref.shape[0] // 2
    source = lax.broadcasted_iota(jnp.int32, (BLOCK, BLOCK), 0)
    target = lax.broadcasted_iota(jnp.int32, (BLOCK, BLOCK), 1)
    edge_row = lax.broadcasted_iota(jnp.int32, (HALO, BLOCK), 0)
    edge = jnp.where(edge_row < HALO // 2, edge_row + BLOCK, edge_row - HALO)
    again = (edge_row >= EDGE) & (edge_row < 3 * EDGE)
    edge_again = jnp.where(edge_row < 2 * EDGE, edge_row - 2 * EDGE, edge_row - 2 * EDGE + BLOCK)
    edge_target = lax.broadcasted_iota(jnp.int32, (HALO, BLOCK), 1)
    for ref, sign in ((wf_ref, 1), (wa_ref, -1)):
        high, low = split(taps_at(sign * (source - target) + frame_radius, frame_ref, 2 * frame_radius + 1))
        edge_high, _ = split(
            taps_at(sign * (edge - edge_target) + frame_radius, frame_ref, 2 * frame_radius + 1)
        )
        _, edge_low = split(
            taps_at(sign * (edge_again - edge_target) + frame_radius, frame_ref, 2 * frame_radius + 1)
        )
        pieces = (high, low, jnp.where(again, edge_low, edge_high), edge_high)
        at = 0
        for piece in pieces:
            ref[at : at + piece.shape[0], :] = piece
            at += piece.shape[0]
    row = lax.broadcasted_iota(jnp.int32, (group, group), 0)
    col = lax.broadcasted_iota(jnp.int32, (group, group), 1)

    def place(index):
        tile, inner = index // 8, index % 8
        scan = (tile // per_lane) * scans + (inner % quads) * per_lane + tile % per_lane
        return scan, inner // quads

    row_scan, row_channel = place(row)
    col_scan, col_channel = place(col)
    for ref, sign in ((sf_ref, 1), (sa_ref, -1)):
        matrix = jnp.where(
            row_channel == col_channel,
            taps_at(sign * (col_scan - row_scan) + scan_radius, scan_ref, 2 * scan_radius + 1),
            0.0,
        )
        high, low = split(matrix)
        ref[0:group, 0:group] = high
        ref[0:group, group : 2 * group] = high
        ref[group : 2 * group, 0:group] = low
        ref[group : 2 * group, group : 2 * group] = jnp.zeros_like(low)


def swap_blocks(tiles, lane, width):
    first, second, third, fourth = tiles
    wide = lane < 2 * width
    narrow = (lane % (2 * width)) < width
    pairs = []
    for a, b in ((first, third), (second, fourth)):
        other = pltpu.roll(jnp.where(wide, b, a), 2 * width, 1)
        pairs.append((jnp.where(wide, a, other), jnp.where(wide, other, b)))
    out = []
    for a, b in zip(pairs[0], pairs[1]):
        out.append(jnp.where(narrow, a, pltpu.roll(b, width, 1)))
        out.append(jnp.where(narrow, pltpu.roll(a, LANES - width, 1), b))
    return out


def deblur_kernel(
    p_ref, sf_ref, sa_ref, wf_ref, wa_ref, out_ref, obs_ref, est_ref, left_ref, back_ref, mean_ref, *, frames, mobs, rows, cells
):
    owners = LANES
    out_rows = out_ref.shape[0] // owners
    units, blocks, group, width = obs_ref.shape
    per_lane = LANES // frames
    lane = lax.broadcasted_iota(jnp.int32, (8, LANES), 1)
    row8 = lax.broadcasted_iota(jnp.int32, (8, 1), 0)
    halo_lane = lax.broadcasted_iota(jnp.int32, (group, HALO), 1)
    halves = width // LANES

    def at(pair, run, y, mob, stride):
        start = ((run * per_lane + y) * mobs + mob) * stride + pair * 8
        return pl.ds(start, 8)

    def scan_blur(values, matrix):
        high, low = split(values)
        return scan_product(matrix, jnp.concatenate([high, low], axis=0))

    def scan_product(matrix, both):
        out = jnp.dot(matrix, both, preferred_element_type=F32)
        return out[0:group] + out[group : 2 * group]

    def put(ref, u, n, values):
        high, low = split(values)
        ref[u, n * group : (n + 1) * group, 0:width] = high
        ref[u, n * group : (n + 1) * group, width : 2 * width] = low

    def put_halo(ref, u):
        zero = jnp.zeros((group, HALO), BF16)
        for n in range(blocks):
            here = slice(n * group, (n + 1) * group)
            for which in (0, 1):
                first = which * width
                after = before = zero
                if n + 1 < blocks:
                    after = ref[u, (n + 1) * group : (n + 2) * group, first : first + HALO]
                if n:
                    before = ref[u, (n - 1) * group : n * group, first + width - HALO : first + width]
                halo = jnp.where(halo_lane < HALO // 2, after, before)
                if which == 0:
                    again = (halo_lane >= EDGE) & (halo_lane < 3 * EDGE)
                    halo = jnp.where(again, pltpu.roll(halo, 2 * EDGE, 1), halo)
                ref[u, here, 2 * width + which * HALO : 2 * width + (which + 1) * HALO] = halo

    def frame_blur(ref, chunks, matrix):
        lhs = []
        for u, first, count in chunks:
            here = slice(first * group, (first + count) * group)
            center, rest = ref[u, here, 0 : 2 * width], ref[u, here, 2 * width : 2 * width + 2 * HALO]
            lhs.append(jnp.concatenate([center, center[:, 0:width], rest], axis=1))
        rhs = jnp.concatenate([matrix[0:width, :], matrix[...]], axis=0)
        out = jnp.dot(jnp.concatenate(lhs, axis=0), rhs, preferred_element_type=F32)
        places = [(u, first + n) for u, first, count in chunks for n in range(count)]
        return [(u, n, out[i * group : (i + 1) * group]) for i, (u, n) in enumerate(places)]

    def total8(parts):
        acc = None
        for part in parts:
            for half in range(halves):
                piece = part[:, half * LANES : (half + 1) * LANES].reshape(group // 8, 8, LANES).sum(axis=0)
                acc = piece if acc is None else acc + piece
        rows_sum = jnp.sum(acc, axis=1, keepdims=True)
        zero = jnp.zeros_like(rows_sum)
        upper = jnp.sum(jnp.where(row8 < 4, rows_sum, zero), axis=0, keepdims=True)
        lower = jnp.sum(jnp.where(row8 < 4, zero, rows_sum), axis=0, keepdims=True)
        return upper, lower

    def gather(u, pair):
        for run in range(blocks * halves):
            n, half = run // halves, run % halves
            for mob in range(mobs):
                tiles = [p_ref[at(pair, run, y, mob, rows), :] for y in range(per_lane)]
                for j, tile in enumerate(swap_blocks(tiles, lane, frames)):
                    b = mob * per_lane + j
                    obs_ref[u, n, b * 8 : b * 8 + 8, half * LANES : (half + 1) * LANES] = tile

    def scatter(u, pair):
        for run in range(blocks * halves):
            n, half = run // halves, run % halves
            for mob in range(mobs):
                tiles = []
                for j in range(per_lane):
                    b = mob * per_lane + j
                    tiles.append(est_ref[u, n, b * 8 : b * 8 + 8, half * LANES : (half + 1) * LANES])
                for y, tile in enumerate(swap_blocks(tiles, lane, frames)):
                    out_ref[at(pair, run, y, mob, out_rows), :] = tile

    def forward(u, iteration):
        estimate = obs_ref if iteration == 0 else est_ref
        for n in range(blocks):
            put(left_ref, u, n, scan_blur(estimate[u, n], sf_ref[...]))
        put_halo(left_ref, u)

    def ratios(chunks):
        for u, n, blurred in frame_blur(left_ref, chunks, wf_ref):
            put(back_ref, u, n, obs_ref[u, n] / blurred)

    def adjoint_frames(chunks):
        for u, n, blurred in frame_blur(back_ref, chunks, wa_ref):
            put(left_ref, u, n, blurred)

    def adjoint_scans(u, iteration):
        estimate = obs_ref if iteration == 0 else est_ref
        for n in range(blocks):
            here = slice(n * group, (n + 1) * group)
            both = jnp.concatenate([left_ref[u, here, 0:width], left_ref[u, here, width : 2 * width]], axis=0)
            est_ref[u, n] = estimate[u, n] * scan_product(sa_ref[...], both)

    def statistics(u, pair):
        upper, lower = total8([est_ref[u, n] for n in range(blocks)])
        upper_mean, lower_mean = upper / cells, lower / cells
        mean8 = jnp.where(row8 < 4, upper_mean, lower_mean)
        squares = []
        for n in range(blocks):
            centered = est_ref[u, n].reshape(group // 8, 8, width) - mean8[None]
            centered = centered.astype(BF16).astype(F32).reshape(group, width)
            squares.append(centered * centered)
        upper_sq, lower_sq = total8(squares)
        upper_inv = 1.0 / jnp.sqrt(upper_sq + 1e-06)
        lower_inv = 1.0 / jnp.sqrt(lower_sq + 1e-06)
        held = mean_ref[...]
        held = jnp.where(lane == 2 * pair, upper_mean, held)
        held = jnp.where(lane == 2 * pair + 1, lower_mean, held)
        held = jnp.where(lane == LANES // 2 + 2 * pair, upper_inv, held)
        held = jnp.where(lane == LANES // 2 + 2 * pair + 1, lower_inv, held)
        mean_ref[...] = held

    members = range(units)
    sets = [[(u, 0, blocks)] for u in members]
    mean_ref[...] = jnp.zeros_like(mean_ref)
    for u in members:
        gather(u, u)
    for iteration in range(ITERS):
        for u in members:
            forward(u, iteration)
        for chunks in sets:
            ratios(chunks)
        for u in members:
            put_halo(back_ref, u)
        for chunks in sets:
            adjoint_frames(chunks)
        for u in members:
            adjoint_scans(u, iteration)
    for u in members:
        statistics(u, u)
        scatter(u, u)
    for owner in range(owners):
        out_ref[owner * out_rows + rows : (owner + 1) * out_rows, :] = mean_ref[0:STATS, :]


def cross_kernel(q_ref, keep_ref, send_ref, centered_ref, *, quads):
    owners = LANES
    stride = q_ref.shape[0] // owners
    core = lax.axis_index("mob") % CORES
    channels = centered_ref.shape[0]
    tiles = channels // LANES
    row_shards, chips, shard_rows, wide = keep_ref.shape
    stats = q_ref[pl.ds(tiles * quads, owners, stride=stride), :]
    stats_t = stats.T
    for k in range(tiles):
        mean = jnp.broadcast_to(stats[:, k : k + 1], (owners, LANES))
        for q in range(quads):
            block = q_ref[pl.ds(k * quads + q, owners, stride=stride), :]
            centered_ref[k * LANES : (k + 1) * LANES, q * LANES : (q + 1) * LANES] = (block - mean).astype(BF16)
    row = jnp.concatenate([stats[:, LANES // 2 + k : LANES // 2 + k + 1] for k in range(PREC // LANES)], axis=0)

    def product(m):
        cross = lax.dot_general(
            centered_ref[:PREC, :],
            centered_ref[PREC + m * wide : PREC + (m + 1) * wide, :],
            (((1,), (1,)), ((), ())),
            preferred_element_type=F32,
        )
        first = LANES // 2 + (PREC + m * wide) // LANES
        column = jnp.concatenate([stats_t[first + i : first + i + 1] for i in range(wide // LANES)], axis=1)
        return (cross * row * column).reshape(row_shards, shard_rows, wide)

    for chip in range(chips):
        even, odd = product(chip * CORES), product(chip * CORES + 1)
        keep_ref[:, chip] = jnp.where(core == 0, even, odd)
        send_ref[:, chip] = jnp.where(core == 0, odd, even)


def finish_kernel(sums_ref, mask_ref, out_ref):
    out_ref[...] = mask_ref[...] * jnp.sum(sums_ref[...], axis=0)


def unpack_kernel(q_ref, est_ref, *, frames, scans):
    owners = LANES
    stride = q_ref.shape[0] // owners
    per_lane = LANES // frames
    quads = scans // per_lane
    tiles = est_ref.shape[0] // (frames * scans)

    def body(k, carry):
        for q in range(quads):
            block = q_ref[pl.ds(k * quads + q, owners, stride=stride), :].T
            for j in range(per_lane):
                est_ref[frame_rows(q * per_lane + j, k, frames, scans, tiles), :] = block[j * frames : (j + 1) * frames]
        return carry

    lax.fori_loop(0, tiles, body, 0)


def local(observed, frame_kernel, scan_kernel, prec_window, frag_window):
    frames, scans, channels = observed.shape
    row_shards, mobs = lax.axis_size("rt"), lax.axis_size("mob")
    owners = row_shards * mobs
    per_lane = LANES // frames
    quads = scans // per_lane
    rows = channels // owners * quads
    group = 8 * per_lane * mobs
    blocks = row_shards * frames // BLOCK
    out_rows = rows + STATS
    width = (channels - PREC) // mobs
    vmem = pl.BlockSpec(memory_space=pltpu.VMEM)
    smem = pl.BlockSpec(memory_space=pltpu.SMEM)
    depth = 2 * BLOCK + 2 * HALO

    hbm = pl.BlockSpec(memory_space=pltpu.HBM)

    def call(kernel, name, out_shape, specs, scratch=(), out_spec=vmem, mib=16.0, micros=5, **statics):
        return pl.pallas_call(
            functools.partial(kernel, **statics),
            out_shape=out_shape,
            in_specs=specs,
            out_specs=jax.tree.map(lambda _: out_spec, out_shape),
            scratch_shapes=scratch,
            compiler_params=pltpu.CompilerParams(vmem_limit_bytes=int(mib * 2**20)),
            cost_estimate=pl.CostEstimate(
                flops=micros * 10**9, bytes_accessed=micros * 3 * 10**6, transcendentals=0
            ),
            name=name,
        )

    shape = jax.ShapeDtypeStruct
    cells = frames * scans
    tiles = channels // LANES
    packed = call(
        pack_kernel,
        "pack",
        shape((owners, rows, LANES), F32),
        [hbm],
        [
            pltpu.VMEM((tiles, cells // 8, 8, LANES), F32),
            pltpu.VMEM((owners * rows, LANES), F32),
            pltpu.SemaphoreType.DMA((tiles,)),
            pltpu.SemaphoreType.DMA((rows // 8,)),
        ],
        out_spec=hbm,
        mib=62,
        frames=frames,
        scans=scans,
    )(to_tiles(observed))
    bands = call(
        bands_kernel,
        "bands",
        (shape((2 * group, 2 * group), BF16),) * 2 + (shape((depth, BLOCK), BF16),) * 2,
        [smem, smem],
        mib=16,
        scans=scans,
        per_lane=per_lane,
    )(frame_kernel, scan_kernel)
    arrived = lax.all_to_all(packed, AXES, 0, 0, tiled=True)
    deblurred = call(
        deblur_kernel,
        "deblur",
        shape((owners * out_rows, LANES), F32),
        [vmem] * 5,
        [
            pltpu.VMEM((rows // 8, blocks, group, BLOCK), F32),
            pltpu.VMEM((rows // 8, blocks, group, BLOCK), F32),
            pltpu.VMEM((rows // 8, blocks * group, 2 * BLOCK + 2 * HALO), BF16),
            pltpu.VMEM((rows // 8, blocks * group, 2 * BLOCK + 2 * HALO), BF16),
            pltpu.VMEM((8, LANES), F32),
        ],
        mib=18,
        frames=frames,
        mobs=mobs,
        rows=rows,
        cells=cells * owners,
    )(arrived.reshape(owners * rows, LANES), *bands)
    returned = lax.all_to_all(
        deblurred.reshape(owners, out_rows // STATS, STATS, LANES), AXES, 0, 0, tiled=True
    ).reshape(owners * out_rows, LANES)
    half = shape((row_shards, mobs // CORES, PREC // row_shards, width), F32)
    keep, send = call(
        cross_kernel, "cross", (half, half), [vmem], [pltpu.VMEM((channels, cells), BF16)], quads=quads
    )(returned)
    both = keep + lax.ppermute(send, "mob", [(m, m ^ 1) for m in range(mobs)])
    groups = [[first + CORES * d for d in range(owners // CORES)] for first in range(CORES)]
    sums = lax.all_to_all(
        both.reshape(owners // CORES, PREC // row_shards, width), AXES, 0, 0, axis_index_groups=groups, tiled=True
    )
    estimate = call(
        unpack_kernel, "unpack", shape((cells * channels // LANES, LANES), F32), [vmem], frames=frames, scans=scans
    )(returned)
    pair_mask = (prec_window[:, None] == frag_window[None, :]).astype(F32)
    correlation = call(finish_kernel, "finish", shape(pair_mask.shape, F32), [vmem] * 2)(sums, pair_mask)
    return from_tiles(estimate, frames, scans), correlation


def solution(mesh):
    placed = (P("rt", "mob", None), P(), P(), P("rt"), P("mob"))
    return jax.shard_map(
        local,
        mesh=mesh,
        in_specs=placed,
        out_specs=(P("rt", "mob", None), P("rt", "mob")),
        check_vma=False,
    )
```
